512 devices in a mesh: gx: 64 (over x, z), gy: 8 (over y, core).
Axes of the slice: x: 4, y: 4, z: 16, core: 2. Of those that a mesh axis runs over, the one named last changes fastest.
Arguments:
- loads: bfloat16 [64, 8, 512, 128], P('gx', 'gy'), may hold values from -16 to 16
- schur: bfloat16 [64, 8, 512, 512], P('gx', 'gy'), may hold values from -0.5 to 3.5, as said below
- local_inverse: bfloat16 [64, 8, 512, 512], P('gx', 'gy'), may hold values from -0.5 to 3.5, as said below
- coarse_basis: float32 [64, 8, 4, 512], P('gx', 'gy'), may hold values from -0.75 to 0.75
- coarse_inverse: float32 [64, 8, 4, 2048], P('gx', 'gy'), may hold values from -0.5 to 2, as said below
- face_map: int32 [64, 8, 512], P('gx', 'gy'), may hold values from 0 to 511, each once within a row
Outputs:
- solution: float32 [64, 8, 512, 128], P('gx', 'gy')
The draws below stay inside these ranges and needn't reach their ends.
Inputs may be any that keep to these rules, and one draw needn't show every extreme that they name: `face_map`: each subdomain's row is a permutation of its 512 interface slots. `schur`: each subdomain's matrix is symmetric and positive definite. `local_inverse`: each subdomain's matrix is symmetric and positive definite. `coarse_inverse`: the whole 2048 x 2048 matrix is symmetric and positive definite.
All inputs are finite; a program needn't handle non-finite values.
Results may differ from the reference program's by a relative error of at most 0.0006.
The reference program's roundings to bfloat16 on the way count: a program that leaves them out, or rounds other values in their place, can miss the bound.
Values sent between devices are 32-bit elements; how exact they have to be, the bound alone decides.
A program may use at most 64 MiB of HBM per device.

```python
import math
import jax
import jax.numpy as jnp
from jax import lax

NI = 512
COLS = 128
NCO = 4
ITERS = 2
FACE = 128
SX = 64
SY = 8
NC = 2048


def symmetric_block(subkey, matrix_order, lowest, highest, spread):
    first_key, second_key = jax.random.split(subkey)
    entries = jnp.clip(jax.random.normal(first_key, (matrix_order, matrix_order), jnp.float32), -4.0, 4.0)
    off_scale = spread / math.sqrt(matrix_order) / 1.4142135
    diagonal = jnp.exp(jax.random.uniform(second_key, (matrix_order,), jnp.float32, math.log(lowest), math.log(highest)))
    return (entries + entries.T) * off_scale + jnp.diag(diagonal)


def subdomain_matrices(key, salt_value, lowest, highest):
    keys_all = jax.random.split(jax.random.fold_in(key, salt_value), SX * SY)

    def single(subkey):
        return symmetric_block(subkey, NI, lowest, highest, 0.6)
    return lax.map(single, keys_all).reshape(SX, SY, NI, NI).astype(jnp.bfloat16)


def draw_schur(key, part):
    return subdomain_matrices(key, 11, 1.5, 3.0)


def draw_local_inverse(key, part):
    return subdomain_matrices(key, 23, 1.5, 3.0)


def draw_coarse_inverse(key, part):
    full_matrix = symmetric_block(jax.random.fold_in(key, 37), NC, 1.0, 1.6, 0.4)
    return full_matrix.reshape(SX, SY, NCO, NC).astype(jnp.float32)


def draw_loads(key, part):
    first_key = jax.random.fold_in(jax.random.fold_in(key, 41), 0)
    ramp_scale = 1.0 + 2.0 * jnp.arange(SX * SY, dtype=jnp.float32) / (SX * SY - 1)
    entries = jnp.clip(jax.random.normal(first_key, (SX * SY, NI, COLS), jnp.float32), -5.0, 5.0)
    return (entries * ramp_scale[:, None, None]).reshape(SX, SY, NI, COLS).astype(jnp.bfloat16)


def block_levels(rng, shape, shards, low, largest):
    def one(axis_at, blocks):
        draws = jax.random.uniform(jax.random.fold_in(jax.random.fold_in(rng, 6), axis_at), (blocks,), jnp.float32, low / len(shards), largest / len(shards))
        return jnp.repeat(jnp.exp(draws), shape[axis_at] // blocks).reshape((-1,) + (1,) * (len(shape) - axis_at - 1))

    factor_of = one(*shards[0])
    for cut in shards[1:]:
        factor_of = factor_of * one(*cut)
    return factor_of


def centred(stream_key, extent, width, most, cuts=(), kind=jnp.bfloat16):
    result = width * jax.random.normal(stream_key, extent, jnp.float32)
    if cuts:
        result = result * block_levels(stream_key, extent, cuts, -0.22, 0.18)
    return jnp.clip(result, -most, most).astype(kind)


def setup_inputs(seed: int = 0) -> dict:
    streams_of = jax.random.split(jax.random.key(seed), 7)
    loads = draw_loads(jax.random.fold_in(streams_of[6], 71), 0)
    schur = draw_schur(jax.random.fold_in(streams_of[6], 71), 0)
    local_inverse = draw_local_inverse(jax.random.fold_in(streams_of[6], 71), 0)
    coarse_basis = centred(streams_of[3], (SX, SY, NCO, NI), 64 ** -0.5, 0.75, ((0, 64), (1, 8)), jnp.float32)
    coarse_inverse = draw_coarse_inverse(jax.random.fold_in(streams_of[6], 71), 0)
    face_map = jax.vmap(lambda own: jax.random.permutation(own, NI))(jax.random.split(streams_of[5], SX * SY)).reshape((SX, SY, NI)).astype(jnp.int32)
    return dict(loads=loads, schur=schur, local_inverse=local_inverse, coarse_basis=coarse_basis, coarse_inverse=coarse_inverse, face_map=face_map)


def face_weights():
    lower_x = jnp.where(jnp.arange(SX) > 0, 0.5, 1.0)
    upper_x = jnp.where(jnp.arange(SX) < SX - 1, 0.5, 1.0)
    lower_y = jnp.where(jnp.arange(SY) > 0, 0.5, 1.0)
    upper_y = jnp.where(jnp.arange(SY) < SY - 1, 0.5, 1.0)
    shape_face = (SX, SY, FACE, 1)
    pieces = [jnp.broadcast_to(lower_x[:, None, None, None], shape_face), jnp.broadcast_to(upper_x[:, None, None, None], shape_face), jnp.broadcast_to(lower_y[None, :, None, None], shape_face), jnp.broadcast_to(upper_y[None, :, None, None], shape_face)]
    return jnp.concatenate(pieces, axis=2).astype(jnp.float32)

def assemble(values):
    west_face = values[:, :, 0:FACE]
    east_face = values[:, :, FACE:2 * FACE]
    south_face = values[:, :, 2 * FACE:3 * FACE]
    north_face = values[:, :, 3 * FACE:]
    blank_x = jnp.zeros_like(west_face[:1])
    blank_y = jnp.zeros_like(south_face[:, :1])
    west_sum = west_face + jnp.concatenate([blank_x, east_face[:-1]], axis=0)
    east_sum = east_face + jnp.concatenate([west_face[1:], blank_x], axis=0)
    south_sum = south_face + jnp.concatenate([blank_y, north_face[:, :-1]], axis=1)
    north_sum = north_face + jnp.concatenate([south_face[:, 1:], blank_y], axis=1)
    return jnp.concatenate([west_sum, east_sum, south_sum, north_sum], axis=2)

def permuted_product(matrices, halves, face_map):

    def single(operands):
        matrix, column_block, index_map = operands
        gathered = column_block[index_map]
        product = jnp.dot(matrix.astype(jnp.float32), gathered.astype(jnp.float32), precision=lax.Precision.HIGHEST, preferred_element_type=jnp.float32)
        return jnp.zeros_like(product).at[index_map].set(product)
    outputs = lax.map(single, (matrices.reshape(SX * SY, NI, NI), halves.reshape(SX * SY, NI, COLS), face_map.reshape(SX * SY, NI)))
    return outputs.reshape(SX, SY, NI, COLS)

def gram(left_mat, right_mat):
    return jnp.einsum('abik,abil->kl', left_mat.astype(jnp.float32), right_mat.astype(jnp.float32), precision=lax.Precision.HIGHEST, preferred_element_type=jnp.float32)

def solve_gram(matrix, right_side):
    factor = jnp.linalg.cholesky(matrix)
    return jax.scipy.linalg.cho_solve((factor, True), right_side)

def times_small(values, small_matrix):
    return jnp.einsum('abik,kl->abil', values.astype(jnp.float32), small_matrix.astype(jnp.float32), precision=lax.Precision.HIGHEST, preferred_element_type=jnp.float32)

def precondition(residual, weights, local_inverse, coarse_basis, coarse_inverse, face_map):
    scaled = weights * residual
    local_part = permuted_product(local_inverse, scaled.astype(jnp.bfloat16), face_map)
    coarse_input = jnp.einsum('abcn,abnk->abck', coarse_basis.astype(jnp.float32), scaled.astype(jnp.float32), precision=lax.Precision.HIGHEST, preferred_element_type=jnp.float32)
    coarse_values = jnp.dot(coarse_inverse.reshape(NC, NC).astype(jnp.float32), coarse_input.reshape(NC, COLS).astype(jnp.float32), precision=lax.Precision.HIGHEST, preferred_element_type=jnp.float32)
    coarse_values = coarse_values.reshape(SX, SY, NCO, COLS)
    correction = local_part + jnp.einsum('abcn,abck->abnk', coarse_basis.astype(jnp.float32), coarse_values.astype(jnp.float32), precision=lax.Precision.HIGHEST, preferred_element_type=jnp.float32)
    return assemble(weights * correction)

def reference(loads, schur, local_inverse, coarse_basis, coarse_inverse, face_map):
    weights = face_weights()
    residual = assemble(loads.astype(jnp.float32))
    solution = jnp.zeros_like(residual)
    update = precondition(residual, weights, local_inverse, coarse_basis, coarse_inverse, face_map)
    precond_gram = gram(residual, weights * update)
    direction = update
    for iteration in range(ITERS):
        image_vec = assemble(permuted_product(schur, direction.astype(jnp.bfloat16), face_map))
        curvature = gram(direction, weights * image_vec)
        step_size = solve_gram(curvature, precond_gram)
        solution = solution + times_small(direction, step_size)
        if iteration + 1 < ITERS:
            residual = residual - times_small(image_vec, step_size)
            update = precondition(residual, weights, local_inverse, coarse_basis, coarse_inverse, face_map)
            next_gram = gram(residual, weights * update)
            ratio_coef = solve_gram(precond_gram, next_gram)
            direction = update + times_small(direction, ratio_coef)
            precond_gram = next_gram
    return solution
```

```python
import functools

import jax
import jax.numpy as jnp
from jax import lax
from jax.experimental import pallas as pl
from jax.experimental.pallas import tpu as pltpu
from jax.sharding import PartitionSpec as P

NZ = 16
MESH = pl.DeviceIdType.MESH
F32 = jnp.float32
BF16 = jnp.bfloat16
HI = lax.Precision.HIGHEST


def mm(a, b):
    return jnp.dot(a, b, precision=HI, preferred_element_type=F32)


def mm_tn(a, b):
    return lax.dot_general(
        a, b, (((0,), (0,)), ((), ())), precision=HI, preferred_element_type=F32
    )


def iota(shape, dim):
    return lax.broadcasted_iota(jnp.int32, shape, dim)


def eliminate(a_ref, g_ref):
    blocks = a_ref.shape[0]
    lanes = a_ref.shape[2]
    sub = iota((8, lanes), 0)

    def step(i, carry):
        pa = a_ref[i]
        pg = g_ref[i]
        for k in range(8):
            col = jnp.broadcast_to(pa[:, k : k + 1], pa.shape)
            inv = 1.0 / jnp.broadcast_to(col[k : k + 1, :], pa.shape)
            ta = jnp.broadcast_to(pa[k : k + 1, :], pa.shape) * inv
            tg = jnp.broadcast_to(pg[k : k + 1, :], pa.shape) * inv
            pa = jnp.where(sub == k, ta, pa - col * ta)
            pg = jnp.where(sub == k, tg, pg - col * tg)
        rows_a = [jnp.broadcast_to(pa[k : k + 1, :], pa.shape) for k in range(8)]
        rows_g = [jnp.broadcast_to(pg[k : k + 1, :], pa.shape) for k in range(8)]
        a_ref[i] = pltpu.roll(pa, lanes - 8, 1)
        g_ref[i] = pg
        for other in range(1, blocks):
            j = lax.rem(i + other, blocks)
            va = a_ref[j]
            vg = g_ref[j]
            cols = [jnp.broadcast_to(va[:, k : k + 1], va.shape) for k in range(8)]
            for k in range(8):
                va = va - cols[k] * rows_a[k]
                vg = vg - cols[k] * rows_g[k]
            a_ref[j] = pltpu.roll(va, lanes - 8, 1)
            g_ref[j] = vg
        return carry

    lax.fori_loop(0, blocks, step, 0)


def kernel(
    nx, nz, ny,
    loads_ref, schur_ref, linv_ref, basis_ref, cinv_ref, map_ref,
    out_ref,
    mp, sp, lf, xr, basis8, c8, cs, c2, cinb, zg, ps, pr, wcs, ims, imgs,
    res, sch, loc, dirs, upd,
    s1, r1, z1s, z1r, g1s, g1r,
    s2, r2, z2s, z2r, g2s, g2r,
    ga, gb, gc,
    xsend, xrecv, psend, precv,
):
    ni, cols = loads_ref.shape
    face = ni // 4
    n_plane = nx * ny
    gx = lax.axis_index("gx")
    gy = lax.axis_index("gy")
    x = gx // nz
    z = lax.rem(gx, nz)
    me = x * ny + gy
    n_gx = nx * nz

    def plane_id(q):
        return ((q // ny) * nz + z, lax.rem(q, ny))

    def line_id(k):
        return (x * nz + k, gy)

    exists = [gx > 0, gx < n_gx - 1, gy > 0, gy < ny - 1]
    nbr = [(gx - 1, gy), (gx + 1, gy), (gx, gy - 1), (gx, gy + 1)]
    w = [jnp.where(e, 0.5, 1.0).astype(F32) for e in exists]

    barrier = pltpu.get_barrier_semaphore()

    def greet_line(o, carry):
        k = lax.rem(z + o, nz)
        pl.semaphore_signal(barrier, inc=1, device_id=line_id(k), device_id_type=MESH)
        return carry

    def greet_plane(o, carry):
        q = lax.rem(me + o, n_plane)
        pl.semaphore_signal(barrier, inc=1, device_id=plane_id(q), device_id_type=MESH)
        return carry

    lax.fori_loop(1, nz, greet_line, 0)
    lax.fori_loop(1, n_plane, greet_plane, 0)
    for f in range(2):
        @pl.when(exists[f])
        def _():
            pl.semaphore_signal(barrier, inc=1, device_id=nbr[f], device_id_type=MESH)

    lf[...] = loads_ref[...].astype(F32)
    for f in range(4):
        @pl.when(jnp.logical_not(exists[f]))
        def _():
            for ph in range(4):
                xr[ph, f] = jnp.zeros((face, cols), F32)
    basis8[...] = jnp.zeros(basis8.shape, F32)
    basis8[0:4, :] = basis_ref[...]
    c8[...] = jnp.zeros(c8.shape, F32)
    c8[0:4, :] = cinv_ref[...]
    if nz < 16:
        zg[...] = jnp.zeros(zg.shape, F32)

    width = nz * ny * 4
    slab = jnp.concatenate([c8[:, i * width : (i + 1) * width] for i in range(nx)], axis=0)
    hi = slab.astype(BF16)
    rest = slab - hi.astype(F32)
    mid = rest.astype(BF16)
    low = (rest - mid.astype(F32)).astype(BF16)
    parts = jnp.concatenate([hi, mid, low], axis=0)
    src = iota((width, 128), 0)
    dst = iota((width, 128), 1)
    src_z, src_y, src_b = src // (ny * 4), lax.rem(src // 4, ny), lax.rem(src, 4)
    want = jnp.where(src_z * 8 + src_b == dst, src_y, -1)
    for q in range(ny):
        pick = jnp.where(want == q, 1.0, 0.0).astype(BF16)
        moved = jnp.dot(parts, pick, preferred_element_type=F32)
        h = 8 * nx
        moved = moved[0:h] + moved[h : 2 * h] + moved[2 * h : 3 * h]
        for i in range(nx):
            cs[i * ny + q] = moved[8 * i : 8 * i + 8]

    onehot = jnp.where(iota((ni, ni), 0) == map_ref[...], 1.0, 0.0).astype(BF16)

    def permuted(matrix):
        right = lax.dot_general(
            matrix, onehot, (((1,), (1,)), ((), ())), preferred_element_type=F32
        ).astype(BF16)
        return jnp.dot(onehot, right, preferred_element_type=F32).astype(BF16)

    mp[...] = permuted(linv_ref[...])
    sp[...] = permuted(schur_ref[...])

    greeted = (nz - 1) + (n_plane - 1) + exists[0].astype(jnp.int32) + exists[1].astype(jnp.int32)
    pl.semaphore_wait(barrier, greeted)

    def face_copy(ph, f, source):
        return pltpu.make_async_remote_copy(
            src_ref=source.at[pl.ds(f * face, face)],
            dst_ref=xr.at[ph, f ^ 1],
            send_sem=xsend.at[ph, f],
            recv_sem=xrecv.at[ph, f ^ 1],
            device_id=nbr[f],
            device_id_type=MESH,
        )

    def face_arrival(ph, f, source):
        return pltpu.make_async_remote_copy(
            src_ref=source.at[pl.ds(f * face, face)],
            dst_ref=xr.at[ph, f],
            send_sem=xsend.at[ph, f],
            recv_sem=xrecv.at[ph, f],
            device_id=nbr[f],
            device_id_type=MESH,
        )

    def faces_start(ph, source):
        for f in range(4):
            @pl.when(exists[f])
            def _():
                face_copy(ph, f, source).start()

    def faces_wait(ph, source):
        for f in range(4):
            @pl.when(exists[f])
            def _():
                face_arrival(ph, f, source).wait_recv()

    def faces_sent(ph, source):
        for f in range(4):
            @pl.when(exists[f])
            def _():
                face_copy(ph, f, source).wait_send()

    def rows(f):
        return slice(f * face, (f + 1) * face)

    def scatter_plane(t, source, target):
        target[me] = source[me]

        def one(o, carry):
            q = lax.rem(me + o, n_plane)
            pltpu.make_async_remote_copy(
                src_ref=source.at[q], dst_ref=target.at[me],
                send_sem=psend.at[t], recv_sem=precv.at[t],
                device_id=plane_id(q), device_id_type=MESH,
            ).start()
            return carry

        lax.fori_loop(1, n_plane, one, 0)

    def spread_plane(t, source, target):
        target[me] = source[...]

        def one(o, carry):
            q = lax.rem(me + o, n_plane)
            pltpu.make_async_remote_copy(
                src_ref=source, dst_ref=target.at[me],
                send_sem=psend.at[t], recv_sem=precv.at[t],
                device_id=plane_id(q), device_id_type=MESH,
            ).start()
            return carry

        lax.fori_loop(1, n_plane, one, 0)

    def spread_line(t, source, target):
        target[z] = source[...]

        def one(o, carry):
            k = lax.rem(z + o, nz)
            pltpu.make_async_remote_copy(
                src_ref=source, dst_ref=target.at[z],
                send_sem=psend.at[t], recv_sem=precv.at[t],
                device_id=line_id(k), device_id_type=MESH,
            ).start()
            return carry

        lax.fori_loop(1, nz, one, 0)

    def arrived(t, target, n):
        part = target.at[pl.ds(0, n - 1)]
        pltpu.make_async_copy(part, part, precv.at[t]).wait()

    def sent(t, target, n):
        part = target.at[pl.ds(0, n - 1)]
        pltpu.make_async_copy(part, part, psend.at[t]).wait()

    def sum_rows(ref):
        return jnp.sum(ref[...], axis=0)

    def coarse_send(it):
        cinb[it] = mm(basis8[...], sch[...])
        spread_line(1 + 2 * it, cinb.at[it], zg.at[it])

    def coarse_turn(it):
        arrived(1 + 2 * it, zg.at[it], nz)
        gathered = zg[it].reshape(zg.shape[1] * 8, cols)
        partial = mm(c2[...].reshape(n_plane * 8, 128), gathered)
        ps[it] = partial.reshape(n_plane, 8, cols)
        scatter_plane(2 + 2 * it, ps.at[it], pr.at[it])

    def coarse_end(it):
        arrived(2 + 2 * it, pr.at[it], n_plane)
        values = sum_rows(pr.at[it])
        loc[...] = loc[...] + mm_tn(basis8[...], values)
        for f in range(4):
            wcs[it, rows(f), :] = w[f] * loc[rows(f), :]

    def reduce_all(t, source, r_ref, zs, zr, gs, gr):
        scatter_plane(t, source, r_ref)
        arrived(t, r_ref, n_plane)
        zs[...] = sum_rows(r_ref)
        spread_line(t + 1, zs, zr)
        arrived(t + 1, zr, nz)
        gs[...] = sum_rows(zr)
        spread_plane(t + 2, gs, gr)
        arrived(t + 2, gr, n_plane)

    def put_gram(target, at, value):
        per = target.shape[1]
        n = 128 // per
        target[at * n : (at + 1) * n] = value.reshape(n, per, 128)

    def get_gram(ref, at):
        n = 128 // ref.shape[1]
        return ref[at * n : (at + 1) * n].reshape(128, 128)

    def to_blocks(v):
        return v.reshape(16, 8, 128)

    faces_start(0, lf)
    scatter_plane(0, cs, c2)

    faces_wait(0, lf)
    for f in range(4):
        res[rows(f), :] = lf[rows(f), :] + xr[0, f]
        sch[rows(f), :] = w[f] * res[rows(f), :]
    coarse_send(0)
    loc[...] = jnp.dot(mp[...], sch[...].astype(BF16), preferred_element_type=F32)
    arrived(0, c2, n_plane)
    coarse_turn(0)
    coarse_end(0)
    faces_start(1, wcs.at[0])
    put_gram(s1, 0, mm_tn(sch[...], loc[...]))
    faces_wait(1, wcs.at[0])
    for f in range(4):
        dirs[rows(f), :] = wcs[0, rows(f), :] + xr[1, f]
    ims[...] = jnp.dot(sp[...], dirs[...].astype(BF16), preferred_element_type=F32)
    faces_start(2, ims)
    put_gram(s1, 1, mm_tn(dirs[...], ims[...]))
    reduce_all(5, s1, r1, z1s, z1r, g1s, g1r)
    faces_wait(2, ims)
    for f in range(4):
        imgs[rows(f), :] = ims[rows(f), :] + xr[2, f]

    gram0 = get_gram(g1r, 0)
    curv = get_gram(g1r, 1)
    ga[...] = to_blocks(0.5 * (curv + curv.T))
    gb[...] = to_blocks(gram0)
    eliminate(ga, gb)
    alpha = gb[...].reshape(128, 128)

    res[...] = res[...] - mm(imgs[...], alpha)
    for f in range(4):
        sch[rows(f), :] = w[f] * res[rows(f), :]
    coarse_send(1)
    loc[...] = jnp.dot(mp[...], sch[...].astype(BF16), preferred_element_type=F32)
    ga[...] = to_blocks(0.5 * (gram0 + gram0.T))
    gc[...] = to_blocks(jnp.where(iota((128, 128), 0) == iota((128, 128), 1), 1.0, 0.0).astype(F32))
    coarse_turn(1)
    eliminate(ga, gc)
    coarse_end(1)
    faces_start(3, wcs.at[1])
    put_gram(s2, 0, mm_tn(sch[...], loc[...]))
    put_gram(s2, 3, jnp.zeros((128, 128), F32))
    faces_wait(3, wcs.at[1])
    for f in range(4):
        upd[rows(f), :] = wcs[1, rows(f), :] + xr[3, f]
    put_gram(s2, 1, mm_tn(upd[...], ims[...]))
    loc[...] = jnp.dot(sp[...], upd[...].astype(BF16), preferred_element_type=F32)
    put_gram(s2, 2, mm_tn(upd[...], loc[...]))
    reduce_all(8, s2, r2, z2s, z2r, g2s, g2r)

    gram1 = get_gram(g2r, 0)
    cross = get_gram(g2r, 1)
    own = get_gram(g2r, 2)
    ratio = mm(gc[...].reshape(128, 128), gram1)
    half_curv = 0.5 * (curv + curv.T)
    side = mm(cross, ratio)
    curv2 = own + side + side.T + mm_tn(ratio, mm(half_curv, ratio))
    ga[...] = to_blocks(0.5 * (curv2 + curv2.T))
    alpha1 = gb[...].reshape(128, 128)
    gb[...] = to_blocks(gram1)
    eliminate(ga, gb)
    step2 = gb[...].reshape(128, 128)
    step1 = alpha1 + mm(ratio, step2)
    out_ref[...] = mm(dirs[...], step1) + mm(upd[...], step2)

    for ph, source in enumerate((lf, wcs.at[0], ims, wcs.at[1])):
        faces_sent(ph, source)
    for it in range(2):
        sent(1 + 2 * it, zg.at[it], nz)
        sent(2 + 2 * it, pr.at[it], n_plane)
    sent(0, c2, n_plane)
    for t, (r_ref, zr, gr) in ((5, (r1, z1r, g1r)), (8, (r2, z2r, g2r))):
        sent(t, r_ref, n_plane)
        sent(t + 1, zr, nz)
        sent(t + 2, gr, n_plane)


def local(nx, nz, ny, loads, schur, local_inverse, coarse_basis, coarse_inverse, face_map):
    ni, cols = loads.shape[2:]
    n_plane = nx * ny
    vm = lambda *shape: pltpu.VMEM(shape, F32)
    face = ni // 4
    p1, p2 = 256 // n_plane, 512 // n_plane
    zslots = max(nz, 16)
    scratch = [
        pltpu.VMEM((ni, ni), BF16), pltpu.VMEM((ni, ni), BF16),
        vm(ni, cols), vm(4, 4, face, cols),
        vm(8, ni), vm(8, coarse_inverse.shape[3]),
        vm(n_plane, 8, 128), vm(n_plane, 8, 128),
        vm(2, 8, cols), vm(2, zslots, 8, cols),
        vm(2, n_plane, 8, cols), vm(2, n_plane, 8, cols),
        vm(2, ni, cols), vm(ni, cols), vm(ni, cols),
        vm(ni, cols), vm(ni, cols), vm(ni, cols), vm(ni, cols), vm(ni, cols),
    ]
    for p in (p1, p2):
        scratch += [
            vm(n_plane, p, cols), vm(n_plane, p, cols),
            vm(p, cols), vm(nz, p, cols),
            vm(p, cols), vm(n_plane, p, cols),
        ]
    scratch += [vm(16, 8, 128)] * 3
    scratch += [
        pltpu.SemaphoreType.DMA((4, 4)), pltpu.SemaphoreType.DMA((4, 4)),
        pltpu.SemaphoreType.DMA((11,)), pltpu.SemaphoreType.DMA((11,)),
    ]
    vmem = pl.BlockSpec(memory_space=pltpu.VMEM)
    out = pl.pallas_call(
        functools.partial(kernel, nx, nz, ny),
        out_shape=jax.ShapeDtypeStruct((ni, cols), F32),
        in_specs=[vmem] * 6,
        out_specs=vmem,
        scratch_shapes=scratch,
        compiler_params=pltpu.CompilerParams(
            collective_id=0, has_side_effects=True, vmem_limit_bytes=48 * 1024 * 1024
        ),
        name="bddc",
    )(
        loads[0, 0], schur[0, 0], local_inverse[0, 0], coarse_basis[0, 0],
        coarse_inverse[0, 0], face_map[0],
    )
    return out[None, None]


def solution(mesh):
    n_gx, ny = mesh.shape["gx"], mesh.shape["gy"]
    return jax.shard_map(
        functools.partial(local, n_gx // NZ, NZ, ny),
        mesh=mesh,
        in_specs=(
            P("gx", "gy", None, None),
            P("gx", "gy", None, None),
            P("gx", "gy", None, None),
            P("gx", "gy", None, None),
            P("gx", "gy", None, None),
            P("gx", "gy", None),
        ),
        out_specs=P("gx", "gy", None, None),
        check_vma=False,
    )
```

```python
import functools

import jax
import jax.numpy as jnp
from jax import lax
from jax.experimental import pallas as pl
from jax.experimental.pallas import tpu as pltpu
from jax.sharding import PartitionSpec as P

NZ = 16
MESH = pl.DeviceIdType.MESH
F32 = jnp.float32
BF16 = jnp.bfloat16
HI = lax.Precision.HIGHEST


def mm(a, b):
    return jnp.dot(a, b, precision=HI, preferred_element_type=F32)


def mm_tn(a, b):
    return lax.dot_general(
        a, b, (((0,), (0,)), ((), ())), precision=HI, preferred_element_type=F32
    )


def iota(shape, dim):
    return lax.broadcasted_iota(jnp.int32, shape, dim)


def split3(v):
    hi = v.astype(BF16)
    rest = v - hi.astype(F32)
    mid = rest.astype(BF16)
    return hi, mid, (rest - mid.astype(F32)).astype(BF16)


def fill_lanes(big):
    spot = iota(big.shape, 0) - 128 == iota(big.shape, 1) // 128
    big[...] = jnp.where(spot, 1.0, 0.0).astype(BF16)


def eliminate(a_ref, g_ref, big, pad):
    sub = iota((8, 128), 0)

    def row(v, s):
        return jnp.broadcast_to(v[s : s + 1, :], (8, 128))

    pad[...] = jnp.zeros(pad.shape, F32)

    def step(i, carry):
        at = pl.multiple_of(i * 16, 16)
        here = pl.ds(at, 16)
        ra = a_ref[here, :]
        rg = g_ref[here, :]
        pick = big[pl.ds(pl.multiple_of(128 - at, 16), 128), :]
        spread = jnp.dot(
            jnp.concatenate(split3(ra), axis=0), pick, preferred_element_type=F32
        )
        spread = spread[0:16] + spread[16:32] + spread[32:48]
        lanes = [
            [spread[8 * h : 8 * h + 8, 128 * j : 128 * j + 128] for h in range(2)]
            for j in range(16)
        ]
        sides = [[ra[0:8], ra[8:16]], [rg[0:8], rg[8:16]]]
        scale = [jnp.ones((8, 128), F32)] * 2
        for k in range(16):
            h, s = divmod(k, 8)
            inv = 1.0 / row(lanes[k][h], s)
            factor = [lanes[k][0] * inv, lanes[k][1] * inv]
            factor[h] = jnp.where(sub == s, 0.0, factor[h])
            scale[h] = jnp.where(sub == s, inv, scale[h])
            for col in lanes[k + 1 :] + sides:
                pivot_row = row(col[h], s)
                for q in range(2):
                    col[q] = col[q] - factor[q] * pivot_row
        pa = jnp.concatenate([sides[0][0] * scale[0], sides[0][1] * scale[1]], axis=0)
        pg = jnp.concatenate([sides[1][0] * scale[0], sides[1][1] * scale[1]], axis=0)
        pad[here, 0:128] = pa
        pad[here, 128:256] = pg
        change = mm(a_ref[...], pad[...])
        a_ref[...] = a_ref[...] - change[:, 0:128]
        g_ref[...] = g_ref[...] - change[:, 128:256]
        a_ref[here, :] = pa
        g_ref[here, :] = pg
        pad[here, :] = jnp.zeros((16, 256), F32)
        return carry

    lax.fori_loop(0, 8, step, 0)


def kernel(
    nx, nz, ny,
    loads_hbm, schur_hbm, linv_hbm, basis_hbm, cinv_hbm, map_hbm,
    out_ref,
    loads_ref, schur_ref, linv_ref, basis_ref, cinv_ref, map_ref, insem,
    mp, sp, lf, xr, basis8, c8, cs, c2, cinb, zg, ps, pr, wcs, ims, imgs,
    res, sch, loc, dirs, upd,
    s1, r1, z1s, z1r, g1s, g1r,
    s2, r2, z2s, z2r, g2s, g2r,
    ga, gb, gc, big, pad,
    xsend, xrecv, psend, precv,
):
    ni, cols = loads_ref.shape
    face = ni // 4
    n_plane = nx * ny
    gx = lax.axis_index("gx")
    gy = lax.axis_index("gy")
    x = gx // nz
    z = lax.rem(gx, nz)
    me = x * ny + gy
    n_gx = nx * nz

    def plane_id(q):
        return ((q // ny) * nz + z, lax.rem(q, ny))

    def line_id(k):
        return (x * nz + k, gy)

    exists = [gx > 0, gx < n_gx - 1, gy > 0, gy < ny - 1]
    nbr = [(gx - 1, gy), (gx + 1, gy), (gx, gy - 1), (gx, gy + 1)]
    w = [jnp.where(e, 0.5, 1.0).astype(F32) for e in exists]

    arrivals = [
        pltpu.make_async_copy(source, target, insem.at[i])
        for i, (source, target) in enumerate((
            (loads_hbm, loads_ref), (cinv_hbm, cinv_ref), (basis_hbm, basis_ref),
            (map_hbm, map_ref), (linv_hbm, linv_ref), (schur_hbm, schur_ref),
        ))
    ]
    for copy in arrivals:
        copy.start()

    barrier = pltpu.get_barrier_semaphore()

    def greet_line(o, carry):
        k = lax.rem(z + o, nz)
        pl.semaphore_signal(barrier, inc=1, device_id=line_id(k), device_id_type=MESH)
        return carry

    def greet_plane(o, carry):
        q = lax.rem(me + o, n_plane)
        pl.semaphore_signal(barrier, inc=1, device_id=plane_id(q), device_id_type=MESH)
        return carry

    lax.fori_loop(1, nz, greet_line, 0)
    lax.fori_loop(1, n_plane, greet_plane, 0)
    for f in range(2):
        @pl.when(exists[f])
        def _():
            pl.semaphore_signal(barrier, inc=1, device_id=nbr[f], device_id_type=MESH)

    fill_lanes(big)
    for copy in arrivals[:4]:
        copy.wait()
    lf[...] = loads_ref[...].astype(F32)
    for f in range(4):
        @pl.when(jnp.logical_not(exists[f]))
        def _():
            for ph in range(4):
                xr[ph, f] = jnp.zeros((face, cols), F32)
    basis8[...] = jnp.zeros(basis8.shape, F32)
    basis8[0:4, :] = basis_ref[...]
    c8[...] = jnp.zeros(c8.shape, F32)
    c8[0:4, :] = cinv_ref[...]
    if nz < 16:
        zg[...] = jnp.zeros(zg.shape, F32)

    width = nz * ny * 4
    slab = jnp.concatenate([c8[:, i * width : (i + 1) * width] for i in range(nx)], axis=0)
    parts = jnp.concatenate(split3(slab), axis=0)
    src = iota((width, 128), 0)
    dst = iota((width, 128), 1)
    src_z, src_y, src_b = src // (ny * 4), lax.rem(src // 4, ny), lax.rem(src, 4)
    want = jnp.where(src_z * 8 + src_b == dst, src_y, -1)
    for q in range(ny):
        pick = jnp.where(want == q, 1.0, 0.0).astype(BF16)
        moved = jnp.dot(parts, pick, preferred_element_type=F32)
        h = 8 * nx
        moved = moved[0:h] + moved[h : 2 * h] + moved[2 * h : 3 * h]
        for i in range(nx):
            cs[i * ny + q] = moved[8 * i : 8 * i + 8]

    onehot = jnp.where(iota((ni, ni), 0) == map_ref[...], 1.0, 0.0).astype(BF16)

    def permuted(matrix):
        right = lax.dot_general(
            matrix, onehot, (((1,), (1,)), ((), ())), preferred_element_type=F32
        ).astype(BF16)
        return jnp.dot(onehot, right, preferred_element_type=F32).astype(BF16)

    arrivals[4].wait()
    mp[...] = permuted(linv_ref[...])
    arrivals[5].wait()
    sp[...] = permuted(schur_ref[...])

    greeted = (nz - 1) + (n_plane - 1) + exists[0].astype(jnp.int32) + exists[1].astype(jnp.int32)
    pl.semaphore_wait(barrier, greeted)

    def face_copy(ph, f, source):
        return pltpu.make_async_remote_copy(
            src_ref=source.at[pl.ds(f * face, face)],
            dst_ref=xr.at[ph, f ^ 1],
            send_sem=xsend.at[ph, f],
            recv_sem=xrecv.at[ph, f ^ 1],
            device_id=nbr[f],
            device_id_type=MESH,
        )

    def face_arrival(ph, f, source):
        return pltpu.make_async_remote_copy(
            src_ref=source.at[pl.ds(f * face, face)],
            dst_ref=xr.at[ph, f],
            send_sem=xsend.at[ph, f],
            recv_sem=xrecv.at[ph, f],
            device_id=nbr[f],
            device_id_type=MESH,
        )

    def faces_start(ph, source):
        for f in range(4):
            @pl.when(exists[f])
            def _():
                face_copy(ph, f, source).start()

    def faces_wait(ph, source):
        for f in range(4):
            @pl.when(exists[f])
            def _():
                face_arrival(ph, f, source).wait_recv()

    def faces_sent(ph, source):
        for f in range(4):
            @pl.when(exists[f])
            def _():
                face_copy(ph, f, source).wait_send()

    def rows(f):
        return slice(f * face, (f + 1) * face)

    def scatter_plane(t, source, target):
        target[me] = source[me]

        def one(o, carry):
            q = lax.rem(me + o, n_plane)
            pltpu.make_async_remote_copy(
                src_ref=source.at[q], dst_ref=target.at[me],
                send_sem=psend.at[t], recv_sem=precv.at[t],
                device_id=plane_id(q), device_id_type=MESH,
            ).start()
            return carry

        lax.fori_loop(1, n_plane, one, 0)

    def spread_plane(t, source, target):
        target[me] = source[...]

        def one(o, carry):
            q = lax.rem(me + o, n_plane)
            pltpu.make_async_remote_copy(
                src_ref=source, dst_ref=target.at[me],
                send_sem=psend.at[t], recv_sem=precv.at[t],
                device_id=plane_id(q), device_id_type=MESH,
            ).start()
            return carry

        lax.fori_loop(1, n_plane, one, 0)

    def spread_line(t, source, target):
        target[z] = source[...]

        def one(o, carry):
            k = lax.rem(z + o, nz)
            pltpu.make_async_remote_copy(
                src_ref=source, dst_ref=target.at[z],
                send_sem=psend.at[t], recv_sem=precv.at[t],
                device_id=line_id(k), device_id_type=MESH,
            ).start()
            return carry

        lax.fori_loop(1, nz, one, 0)

    def arrived(t, target, n):
        part = target.at[pl.ds(0, n - 1)]
        pltpu.make_async_copy(part, part, precv.at[t]).wait()

    def sent(t, target, n):
        part = target.at[pl.ds(0, n - 1)]
        pltpu.make_async_copy(part, part, psend.at[t]).wait()

    def sum_rows(ref):
        return jnp.sum(ref[...], axis=0)

    def coarse_send(it):
        cinb[it] = mm(basis8[...], sch[...])
        spread_line(1 + 2 * it, cinb.at[it], zg.at[it])

    def coarse_turn(it):
        arrived(1 + 2 * it, zg.at[it], nz)
        gathered = zg[it].reshape(zg.shape[1] * 8, cols)
        partial = mm(c2[...].reshape(n_plane * 8, 128), gathered)
        ps[it] = partial.reshape(n_plane, 8, cols)
        scatter_plane(2 + 2 * it, ps.at[it], pr.at[it])

    def coarse_end(it):
        arrived(2 + 2 * it, pr.at[it], n_plane)
        values = sum_rows(pr.at[it])
        loc[...] = loc[...] + mm_tn(basis8[...], values)
        for f in range(4):
            wcs[it, rows(f), :] = w[f] * loc[rows(f), :]

    def reduce_all(t, source, r_ref, zs, zr, gs, gr):
        scatter_plane(t, source, r_ref)
        arrived(t, r_ref, n_plane)
        zs[...] = sum_rows(r_ref)
        spread_line(t + 1, zs, zr)
        arrived(t + 1, zr, nz)
        gs[...] = sum_rows(zr)
        spread_plane(t + 2, gs, gr)
        arrived(t + 2, gr, n_plane)

    def put_gram(target, at, value):
        per = target.shape[1]
        n = 128 // per
        target[at * n : (at + 1) * n] = value.reshape(n, per, 128)

    def get_gram(ref, at):
        n = 128 // ref.shape[1]
        return ref[at * n : (at + 1) * n].reshape(128, 128)

    faces_start(0, lf)
    scatter_plane(0, cs, c2)

    faces_wait(0, lf)
    for f in range(4):
        res[rows(f), :] = lf[rows(f), :] + xr[0, f]
        sch[rows(f), :] = w[f] * res[rows(f), :]
    coarse_send(0)
    loc[...] = jnp.dot(mp[...], sch[...].astype(BF16), preferred_element_type=F32)
    arrived(0, c2, n_plane)
    coarse_turn(0)
    coarse_end(0)
    faces_start(1, wcs.at[0])
    put_gram(s1, 0, mm_tn(sch[...], loc[...]))
    faces_wait(1, wcs.at[0])
    for f in range(4):
        dirs[rows(f), :] = wcs[0, rows(f), :] + xr[1, f]
    ims[...] = jnp.dot(sp[...], dirs[...].astype(BF16), preferred_element_type=F32)
    faces_start(2, ims)
    put_gram(s1, 1, mm_tn(dirs[...], ims[...]))
    reduce_all(5, s1, r1, z1s, z1r, g1s, g1r)
    faces_wait(2, ims)
    for f in range(4):
        imgs[rows(f), :] = ims[rows(f), :] + xr[2, f]

    gram0 = get_gram(g1r, 0)
    curv = get_gram(g1r, 1)
    ga[...] = 0.5 * (curv + curv.T)
    gb[...] = gram0
    eliminate(ga, gb, big, pad)
    alpha = gb[...]

    res[...] = res[...] - mm(imgs[...], alpha)
    for f in range(4):
        sch[rows(f), :] = w[f] * res[rows(f), :]
    coarse_send(1)
    loc[...] = jnp.dot(mp[...], sch[...].astype(BF16), preferred_element_type=F32)
    ga[...] = 0.5 * (gram0 + gram0.T)
    gc[...] = jnp.where(iota((128, 128), 0) == iota((128, 128), 1), 1.0, 0.0).astype(F32)
    eliminate(ga, gc, big, pad)
    coarse_turn(1)
    coarse_end(1)
    faces_start(3, wcs.at[1])
    put_gram(s2, 0, mm_tn(sch[...], loc[...]))
    put_gram(s2, 3, jnp.zeros((128, 128), F32))
    faces_wait(3, wcs.at[1])
    for f in range(4):
        upd[rows(f), :] = wcs[1, rows(f), :] + xr[3, f]
    put_gram(s2, 1, mm_tn(upd[...], ims[...]))
    loc[...] = jnp.dot(sp[...], upd[...].astype(BF16), preferred_element_type=F32)
    put_gram(s2, 2, mm_tn(upd[...], loc[...]))
    reduce_all(8, s2, r2, z2s, z2r, g2s, g2r)

    gram1 = get_gram(g2r, 0)
    cross = get_gram(g2r, 1)
    own = get_gram(g2r, 2)
    ratio = mm(gc[...], gram1)
    half_curv = 0.5 * (curv + curv.T)
    side = mm(cross, ratio)
    curv2 = own + side + side.T + mm_tn(ratio, mm(half_curv, ratio))
    ga[...] = 0.5 * (curv2 + curv2.T)
    alpha1 = gb[...]
    gb[...] = gram1
    eliminate(ga, gb, big, pad)
    step2 = gb[...]
    step1 = alpha1 + mm(ratio, step2)
    out_ref[...] = mm(dirs[...], step1) + mm(upd[...], step2)

    for ph, source in enumerate((lf, wcs.at[0], ims, wcs.at[1])):
        faces_sent(ph, source)
    for it in range(2):
        sent(1 + 2 * it, zg.at[it], nz)
        sent(2 + 2 * it, pr.at[it], n_plane)
    sent(0, c2, n_plane)
    for t, (r_ref, zr, gr) in ((5, (r1, z1r, g1r)), (8, (r2, z2r, g2r))):
        sent(t, r_ref, n_plane)
        sent(t + 1, zr, nz)
        sent(t + 2, gr, n_plane)


def local(nx, nz, ny, loads, schur, local_inverse, coarse_basis, coarse_inverse, face_map):
    ni, cols = loads.shape[2:]
    n_plane = nx * ny
    vm = lambda *shape: pltpu.VMEM(shape, F32)
    face = ni // 4
    p1, p2 = 256 // n_plane, 512 // n_plane
    zslots = max(nz, 16)
    scratch = [
        pltpu.VMEM((ni, cols), BF16), pltpu.VMEM((ni, ni), BF16), pltpu.VMEM((ni, ni), BF16),
        vm(4, ni), vm(4, coarse_inverse.shape[3]), pltpu.VMEM((1, ni), jnp.int32),
        pltpu.SemaphoreType.DMA((6,)),
        pltpu.VMEM((ni, ni), BF16), pltpu.VMEM((ni, ni), BF16),
        vm(ni, cols), vm(4, 4, face, cols),
        vm(8, ni), vm(8, coarse_inverse.shape[3]),
        vm(n_plane, 8, 128), vm(n_plane, 8, 128),
        vm(2, 8, cols), vm(2, zslots, 8, cols),
        vm(2, n_plane, 8, cols), vm(2, n_plane, 8, cols),
        vm(2, ni, cols), vm(ni, cols), vm(ni, cols),
        vm(ni, cols), vm(ni, cols), vm(ni, cols), vm(ni, cols), vm(ni, cols),
    ]
    for p in (p1, p2):
        scratch += [
            vm(n_plane, p, cols), vm(n_plane, p, cols),
            vm(p, cols), vm(nz, p, cols),
            vm(p, cols), vm(n_plane, p, cols),
        ]
    scratch += [vm(128, 128)] * 3 + [pltpu.VMEM((256, 2048), BF16), vm(128, 256)]
    scratch += [
        pltpu.SemaphoreType.DMA((4, 4)), pltpu.SemaphoreType.DMA((4, 4)),
        pltpu.SemaphoreType.DMA((11,)), pltpu.SemaphoreType.DMA((11,)),
    ]
    vmem = pl.BlockSpec(memory_space=pltpu.VMEM)
    out = pl.pallas_call(
        functools.partial(kernel, nx, nz, ny),
        out_shape=jax.ShapeDtypeStruct((ni, cols), F32),
        in_specs=[pl.BlockSpec(memory_space=pltpu.HBM)] * 6,
        out_specs=vmem,
        scratch_shapes=scratch,
        compiler_params=pltpu.CompilerParams(
            collective_id=0, has_side_effects=True, vmem_limit_bytes=67_000_000
        ),
        name="bddc",
    )(
        loads[0, 0], schur[0, 0], local_inverse[0, 0], coarse_basis[0, 0],
        coarse_inverse[0, 0], face_map[0],
    )
    return out[None, None]


def solution(mesh):
    n_gx, ny = mesh.shape["gx"], mesh.shape["gy"]
    return jax.shard_map(
        functools.partial(local, n_gx // NZ, NZ, ny),
        mesh=mesh,
        in_specs=(
            P("gx", "gy", None, None),
            P("gx", "gy", None, None),
            P("gx", "gy", None, None),
            P("gx", "gy", None, None),
            P("gx", "gy", None, None),
            P("gx", "gy", None),
        ),
        out_specs=P("gx", "gy", None, None),
        check_vma=False,
    )
```

```python
import functools

import jax
import jax.numpy as jnp
from jax import lax
from jax.experimental import pallas as pl
from jax.experimental.pallas import tpu as pltpu
from jax.sharding import PartitionSpec as P

NZ = 16
MESH = pl.DeviceIdType.MESH
F32 = jnp.float32
BF16 = jnp.bfloat16
HI = lax.Precision.HIGHEST


def mm(a, b):
    return jnp.dot(a, b, precision=HI, preferred_element_type=F32)


def mm_tn(a, b):
    return lax.dot_general(
        a, b, (((0,), (0,)), ((), ())), precision=HI, preferred_element_type=F32
    )


def iota(shape, dim):
    return lax.broadcasted_iota(jnp.int32, shape, dim)


def split3(v):
    hi = v.astype(BF16)
    rest = v - hi.astype(F32)
    mid = rest.astype(BF16)
    return hi, mid, (rest - mid.astype(F32)).astype(BF16)


def fill_lanes(big):
    spot = iota(big.shape, 0) - 128 == iota(big.shape, 1) // 128
    big[...] = jnp.where(spot, 1.0, 0.0).astype(BF16)


def eliminate(a_ref, g_ref, big, pad):
    sub = iota((8, 128), 0)

    def row(v, s):
        return jnp.broadcast_to(v[s : s + 1, :], (8, 128))

    pad[...] = jnp.zeros(pad.shape, F32)

    def step(i, carry):
        at = pl.multiple_of(i * 16, 16)
        here = pl.ds(at, 16)
        ra = a_ref[here, :]
        rg = g_ref[here, :]
        pick = big[pl.ds(pl.multiple_of(128 - at, 16), 128), :]
        spread = jnp.dot(
            jnp.concatenate(split3(ra), axis=0), pick, preferred_element_type=F32
        )
        spread = spread[0:16] + spread[16:32] + spread[32:48]
        lanes = [
            [spread[8 * h : 8 * h + 8, 128 * j : 128 * j + 128] for h in range(2)]
            for j in range(16)
        ]
        sides = [[ra[0:8], ra[8:16]], [rg[0:8], rg[8:16]]]
        scale = [jnp.ones((8, 128), F32)] * 2
        for k in range(16):
            h, s = divmod(k, 8)
            inv = 1.0 / row(lanes[k][h], s)
            factor = [lanes[k][0] * inv, lanes[k][1] * inv]
            factor[h] = jnp.where(sub == s, 0.0, factor[h])
            scale[h] = jnp.where(sub == s, inv, scale[h])
            for col in lanes[k + 1 :] + sides:
                pivot_row = row(col[h], s)
                for q in range(2):
                    col[q] = col[q] - factor[q] * pivot_row
        pa = jnp.concatenate([sides[0][0] * scale[0], sides[0][1] * scale[1]], axis=0)
        pg = jnp.concatenate([sides[1][0] * scale[0], sides[1][1] * scale[1]], axis=0)
        pad[here, 0:128] = pa
        pad[here, 128:256] = pg
        change = mm(a_ref[...], pad[...])
        a_ref[...] = a_ref[...] - change[:, 0:128]
        g_ref[...] = g_ref[...] - change[:, 128:256]
        a_ref[here, :] = pa
        g_ref[here, :] = pg
        pad[here, :] = jnp.zeros((16, 256), F32)
        return carry

    lax.fori_loop(0, 8, step, 0)


def kernel(
    nx, nz, ny,
    loads_hbm, schur_hbm, linv_hbm, basis_hbm, cinv_hbm, map_hbm,
    out_ref,
    loads_ref, schur_ref, linv_ref, basis_ref, cinv_ref, map_ref, insem,
    mp, sp, lf, xr, basis8, c8, cs, c2, cinb, zg, ps, pr, wcs, ims, imgs,
    res, sch, loc, dirs, upd,
    gsrc, gparts, gmine, gline, gtotal, gresult,
    ga, gb, gc, gd, ge, cval, big, pad,
    xsend, xrecv, psend, precv,
):
    ni, cols = loads_ref.shape
    face = ni // 4
    n_plane = nx * ny
    gx = lax.axis_index("gx")
    gy = lax.axis_index("gy")
    x = gx // nz
    z = lax.rem(gx, nz)
    me = x * ny + gy
    n_gx = nx * nz
    nyc = ny // 2

    def plane_id(q):
        return ((q // ny) * nz + z, lax.rem(q, ny))

    def line_id(k):
        return (x * nz + k, gy)

    exists = [gx > 0, gx < n_gx - 1, gy > 0, gy < ny - 1]
    nbr = [(gx - 1, gy), (gx + 1, gy), (gx, gy - 1), (gx, gy + 1)]
    w = [jnp.where(e, 0.5, 1.0).astype(F32) for e in exists]

    arrivals = [
        pltpu.make_async_copy(source, target, insem.at[i])
        for i, (source, target) in enumerate((
            (loads_hbm, loads_ref), (cinv_hbm, cinv_ref), (basis_hbm, basis_ref),
            (map_hbm, map_ref), (linv_hbm, linv_ref), (schur_hbm, schur_ref),
        ))
    ]
    for copy in arrivals:
        copy.start()

    barrier = pltpu.get_barrier_semaphore()

    def greet_line(o, carry):
        k = lax.rem(z + o, nz)
        pl.semaphore_signal(barrier, inc=1, device_id=line_id(k), device_id_type=MESH)
        return carry

    def greet_plane(o, carry):
        q = lax.rem(me + o, n_plane)
        pl.semaphore_signal(barrier, inc=1, device_id=plane_id(q), device_id_type=MESH)
        return carry

    lax.fori_loop(1, nz, greet_line, 0)
    lax.fori_loop(1, n_plane, greet_plane, 0)
    for f in range(2):
        @pl.when(exists[f])
        def _():
            pl.semaphore_signal(barrier, inc=1, device_id=nbr[f], device_id_type=MESH)

    fill_lanes(big)
    for copy in arrivals[:4]:
        copy.wait()
    lf[...] = loads_ref[...].astype(F32)
    for f in range(4):
        @pl.when(jnp.logical_not(exists[f]))
        def _():
            for ph in range(4):
                xr[ph, f] = jnp.zeros((face, cols), F32)
    basis8[...] = jnp.zeros(basis8.shape, F32)
    basis8[0:4, :] = basis_ref[...]
    c8[...] = jnp.zeros(c8.shape, F32)
    c8[0:4, :] = cinv_ref[...]
    if nz < 16:
        zg[...] = jnp.zeros(zg.shape, F32)

    width = nz * ny * 4
    slab = jnp.concatenate([c8[:, i * width : (i + 1) * width] for i in range(nx)], axis=0)
    parts = jnp.concatenate(split3(slab), axis=0)
    src = iota((width, 128), 0)
    dst = iota((width, 128), 1)
    src_z, src_y, src_b = src // (ny * 4), lax.rem(src // 4, ny), lax.rem(src, 4)
    want = jnp.where(src_z * 8 + src_b == dst, src_y, -1)
    for q in range(ny):
        pick = jnp.where(want == q, 1.0, 0.0).astype(BF16)
        moved = jnp.dot(parts, pick, preferred_element_type=F32)
        h = 8 * nx
        moved = moved[0:h] + moved[h : 2 * h] + moved[2 * h : 3 * h]
        for i in range(nx):
            cs[i * ny + q] = moved[8 * i : 8 * i + 8]

    onehot = jnp.where(iota((ni, ni), 0) == map_ref[...], 1.0, 0.0).astype(BF16)

    def permuted(matrix):
        right = lax.dot_general(
            matrix, onehot, (((1,), (1,)), ((), ())), preferred_element_type=F32
        ).astype(BF16)
        return jnp.dot(onehot, right, preferred_element_type=F32).astype(BF16)

    arrivals[4].wait()
    mp[...] = permuted(linv_ref[...])
    arrivals[5].wait()
    sp[...] = permuted(schur_ref[...])

    greeted = (nz - 1) + (n_plane - 1) + exists[0].astype(jnp.int32) + exists[1].astype(jnp.int32)
    pl.semaphore_wait(barrier, greeted)

    def face_copy(ph, f, source):
        return pltpu.make_async_remote_copy(
            src_ref=source.at[pl.ds(f * face, face)],
            dst_ref=xr.at[ph, f ^ 1],
            send_sem=xsend.at[ph, f],
            recv_sem=xrecv.at[ph, f ^ 1],
            device_id=nbr[f],
            device_id_type=MESH,
        )

    def face_arrival(ph, f, source):
        return pltpu.make_async_remote_copy(
            src_ref=source.at[pl.ds(f * face, face)],
            dst_ref=xr.at[ph, f],
            send_sem=xsend.at[ph, f],
            recv_sem=xrecv.at[ph, f],
            device_id=nbr[f],
            device_id_type=MESH,
        )

    def faces_start(ph, source):
        for f in range(4):
            @pl.when(exists[f])
            def _():
                face_copy(ph, f, source).start()

    def faces_wait(ph, source):
        for f in range(4):
            @pl.when(exists[f])
            def _():
                face_arrival(ph, f, source).wait_recv()

    def faces_sent(ph, source):
        for f in range(4):
            @pl.when(exists[f])
            def _():
                face_copy(ph, f, source).wait_send()

    def rows(f):
        return slice(f * face, (f + 1) * face)

    def wrap(v, n):
        return lax.rem(v, n)

    core = lax.rem(gy, 2)
    chip_y = gy // 2
    ys = [wrap(chip_y + o, nyc) for o in range(nyc)]
    far_y = [nyc // 2] + [o for o in range(nyc) if o not in (0, nyc // 2)] + [0]
    far_y = far_y if nyc > 1 else [0]

    def over_plane(send):
        def one(k, carry):
            xo = wrap(x + 1 + k, nx)
            for o in far_y:
                for d in (1, 0):
                    send(xo, ys[o], wrap(core + d, 2))
            return carry

        lax.fori_loop(0, nx - 1, one, 0)
        for o in far_y:
            for d in (1, 0):
                if o or d:
                    send(x, ys[o], wrap(core + d, 2))

    def over_chips(send):
        def one(k, carry):
            xo = wrap(x + 1 + k, nx)
            for o in far_y:
                send(xo, ys[o])
            return carry

        lax.fori_loop(0, nx - 1, one, 0)
        for o in far_y:
            if o:
                send(x, ys[o])

    def over_line(send):
        send(wrap(z + nz // 2, nz))

        def one(k, carry):
            d = nz // 2 - 1 - k
            send(wrap(z + d, nz))
            send(wrap(z + nz - d, nz))
            return carry

        lax.fori_loop(0, nz // 2 - 1, one, 0)

    def push(t, source, target, device):
        pltpu.make_async_remote_copy(
            src_ref=source, dst_ref=target,
            send_sem=psend.at[t], recv_sem=precv.at[t],
            device_id=device, device_id_type=MESH,
        ).start()

    def scatter_plane(t, source, target):
        target[me] = source[me]

        def send(xo, yo, co):
            q = xo * ny + yo * 2 + co
            push(t, source.at[q], target.at[me], (xo * nz + z, yo * 2 + co))

        over_plane(send)

    def spread_line(t, source, target):
        target[z] = source[...]
        over_line(lambda k: push(t, source, target.at[z], (x * nz + k, gy)))

    def arrived(t, target, n):
        part = target.at[pl.ds(0, n)]
        pltpu.make_async_copy(part, part, precv.at[t]).wait()

    def sent(t, target, n):
        part = target.at[pl.ds(0, n)]
        pltpu.make_async_copy(part, part, psend.at[t]).wait()

    n_tiles = n_plane // 2
    my_tile = x * nyc + chip_y

    class Sum:
        def __init__(self, r, parity):
            self.t = 5 + 3 * r
            self.parity = parity
            self.src, self.parts = gsrc.at[r], gparts.at[r]
            self.mine, self.line_parts = gmine.at[r], gline.at[r]
            self.total, self.result = gtotal.at[r], gresult.at[r]
            self.owner = core == parity

        def scatter(self, matrix):
            self.src[...] = matrix.reshape(n_tiles, 128 // n_tiles, 128)

            @pl.when(self.owner)
            def _():
                self.parts[me] = self.src[my_tile]

            def send(xo, yo):
                push(
                    self.t, self.src.at[xo * nyc + yo], self.parts.at[me],
                    (xo * nz + z, yo * 2 + self.parity),
                )

            over_chips(send)

            @pl.when(jnp.logical_not(self.owner))
            def _():
                send(x, chip_y)

        def line(self):
            @pl.when(self.owner)
            def _():
                arrived(self.t, self.parts, n_plane - 1)
                self.mine[...] = sum_rows(self.parts)
                spread_line(self.t + 1, self.mine, self.line_parts)

        def spread(self):
            @pl.when(self.owner)
            def _():
                arrived(self.t + 1, self.line_parts, nz - 1)
                self.total[...] = sum_rows(self.line_parts)
                self.result[my_tile] = self.total[...]
                over_plane(
                    lambda xo, yo, co: push(
                        self.t + 2, self.total, self.result.at[my_tile],
                        (xo * nz + z, yo * 2 + co),
                    )
                )

        def finish(self):
            @pl.when(self.owner)
            def _():
                if n_tiles > 1:
                    arrived(self.t + 2, self.result, n_tiles - 1)

            @pl.when(jnp.logical_not(self.owner))
            def _():
                arrived(self.t + 2, self.result, n_tiles)

            return self.result[...].reshape(128, 128)

        def drain(self):
            @pl.when(self.owner)
            def _():
                sent(self.t, self.parts, n_tiles - 1)
                sent(self.t + 1, self.line_parts, nz - 1)
                sent(self.t + 2, self.parts, n_plane - 1)

            @pl.when(jnp.logical_not(self.owner))
            def _():
                sent(self.t, self.parts, n_tiles)

    def sum_rows(ref):
        return jnp.sum(ref[...], axis=0)

    def coarse_send(it):
        cinb[it] = mm(basis8[...], sch[...])
        spread_line(1 + 2 * it, cinb.at[it], zg.at[it])

    def coarse_turn(it):
        arrived(1 + 2 * it, zg.at[it], nz - 1)
        gathered = zg[it].reshape(zg.shape[1] * 8, cols)
        partial = mm(c2[...].reshape(n_plane * 8, 128), gathered)
        ps[it] = partial.reshape(n_plane, 8, cols)
        scatter_plane(2 + 2 * it, ps.at[it], pr.at[it])

    def coarse_values(it):
        arrived(2 + 2 * it, pr.at[it], n_plane - 1)
        return sum_rows(pr.at[it])

    def correct(it, values):
        loc[...] = loc[...] + mm_tn(basis8[...], values)
        for f in range(4):
            wcs[it, rows(f), :] = w[f] * loc[rows(f), :]
        faces_start(1 + 2 * it, wcs.at[it])

    def symmetric(v):
        return 0.5 * (v + v.T)

    first_gram, first_curv = Sum(0, 0), Sum(1, 1)
    next_gram, cross_gram, own_curv = Sum(2, 0), Sum(3, 1), Sum(4, 0)

    faces_start(0, lf)
    scatter_plane(0, cs, c2)
    faces_wait(0, lf)
    for f in range(4):
        res[rows(f), :] = lf[rows(f), :] + xr[0, f]
        sch[rows(f), :] = w[f] * res[rows(f), :]
    coarse_send(0)
    loc[...] = jnp.dot(mp[...], sch[...].astype(BF16), preferred_element_type=F32)
    arrived(0, c2, n_plane - 1)
    coarse_turn(0)
    values0 = coarse_values(0)
    correct(0, values0)
    cval[...] = values0
    first_gram.scatter(mm_tn(sch[...], loc[...]))
    faces_wait(1, wcs.at[0])
    for f in range(4):
        dirs[rows(f), :] = wcs[0, rows(f), :] + xr[1, f]
    ims[...] = jnp.dot(sp[...], dirs[...].astype(BF16), preferred_element_type=F32)
    faces_start(2, ims)
    first_curv.scatter(mm_tn(dirs[...], ims[...]))

    first_gram.line()
    faces_wait(2, ims)
    for f in range(4):
        imgs[rows(f), :] = ims[rows(f), :] + xr[2, f]
        sch[rows(f), :] = w[f] * imgs[rows(f), :]
    coarse_send(1)
    first_curv.line()
    first_gram.spread()
    coarse_turn(1)
    first_curv.spread()
    gram0 = first_gram.finish()
    gb[...] = gram0
    ge[...] = symmetric(gram0)
    gc[...] = jnp.where(iota((128, 128), 0) == iota((128, 128), 1), 1.0, 0.0).astype(F32)
    image_values = coarse_values(1)
    half_curv = symmetric(first_curv.finish())
    gd[...] = half_curv
    ga[...] = half_curv
    eliminate(ga, gb, big, pad)
    alpha = gb[...]

    res[...] = res[...] - mm(imgs[...], alpha)
    for f in range(4):
        sch[rows(f), :] = w[f] * res[rows(f), :]
    loc[...] = jnp.dot(mp[...], sch[...].astype(BF16), preferred_element_type=F32)
    correct(1, cval[...] - mm(image_values, alpha))
    next_gram.scatter(mm_tn(sch[...], loc[...]))
    faces_wait(3, wcs.at[1])
    for f in range(4):
        upd[rows(f), :] = wcs[1, rows(f), :] + xr[3, f]
    cross_gram.scatter(mm_tn(upd[...], ims[...]))
    loc[...] = jnp.dot(sp[...], upd[...].astype(BF16), preferred_element_type=F32)
    own_curv.scatter(mm_tn(upd[...], loc[...]))
    next_gram.line()
    cross_gram.line()
    own_curv.line()
    eliminate(ge, gc, big, pad)
    next_gram.spread()
    cross_gram.spread()
    own_curv.spread()

    gram1 = next_gram.finish()
    ratio = mm(gc[...], gram1)
    known = mm_tn(ratio, mm(gd[...], ratio))
    step1 = gb[...]
    gb[...] = gram1
    side = mm(cross_gram.finish(), ratio)
    ga[...] = symmetric(own_curv.finish() + side + side.T + known)
    eliminate(ga, gb, big, pad)
    step2 = gb[...]
    step1 = step1 + mm(ratio, step2)
    out_ref[...] = mm(dirs[...], step1) + mm(upd[...], step2)

    for ph, source in enumerate((lf, wcs.at[0], ims, wcs.at[1])):
        faces_sent(ph, source)
    for it in range(2):
        sent(1 + 2 * it, zg.at[it], nz - 1)
        sent(2 + 2 * it, pr.at[it], n_plane - 1)
    sent(0, c2, n_plane - 1)
    for item in (first_gram, first_curv, next_gram, cross_gram, own_curv):
        item.drain()


def local(nx, nz, ny, loads, schur, local_inverse, coarse_basis, coarse_inverse, face_map):
    ni, cols = loads.shape[2:]
    n_plane = nx * ny
    vm = lambda *shape: pltpu.VMEM(shape, F32)
    face = ni // 4
    n_tiles = n_plane // 2
    tile = 128 // n_tiles
    zslots = max(nz, 16)
    scratch = [
        pltpu.VMEM((ni, cols), BF16), pltpu.VMEM((ni, ni), BF16), pltpu.VMEM((ni, ni), BF16),
        vm(4, ni), vm(4, coarse_inverse.shape[3]), pltpu.VMEM((1, ni), jnp.int32),
        pltpu.SemaphoreType.DMA((6,)),
        pltpu.VMEM((ni, ni), BF16), pltpu.VMEM((ni, ni), BF16),
        vm(ni, cols), vm(4, 4, face, cols),
        vm(8, ni), vm(8, coarse_inverse.shape[3]),
        vm(n_plane, 8, 128), vm(n_plane, 8, 128),
        vm(2, 8, cols), vm(2, zslots, 8, cols),
        vm(2, n_plane, 8, cols), vm(2, n_plane, 8, cols),
        vm(2, ni, cols), vm(ni, cols), vm(ni, cols),
        vm(ni, cols), vm(ni, cols), vm(ni, cols), vm(ni, cols), vm(ni, cols),
    ]
    scratch += [
        vm(5, n_tiles, tile, cols), vm(5, n_plane, tile, cols), vm(5, tile, cols),
        vm(5, nz, tile, cols), vm(5, tile, cols), vm(5, n_tiles, tile, cols),
    ]
    scratch += [vm(128, 128)] * 5 + [vm(8, cols), pltpu.VMEM((256, 2048), BF16), vm(128, 256)]
    scratch += [
        pltpu.SemaphoreType.DMA((4, 4)), pltpu.SemaphoreType.DMA((4, 4)),
        pltpu.SemaphoreType.DMA((20,)), pltpu.SemaphoreType.DMA((20,)),
    ]
    vmem = pl.BlockSpec(memory_space=pltpu.VMEM)
    out = pl.pallas_call(
        functools.partial(kernel, nx, nz, ny),
        out_shape=jax.ShapeDtypeStruct((ni, cols), F32),
        in_specs=[pl.BlockSpec(memory_space=pltpu.HBM)] * 6,
        out_specs=vmem,
        scratch_shapes=scratch,
        compiler_params=pltpu.CompilerParams(
            collective_id=0, has_side_effects=True, vmem_limit_bytes=67_000_000
        ),
        name="bddc",
    )(
        loads[0, 0], schur[0, 0], local_inverse[0, 0], coarse_basis[0, 0],
        coarse_inverse[0, 0], face_map[0],
    )
    return out[None, None]


def solution(mesh):
    n_gx, ny = mesh.shape["gx"], mesh.shape["gy"]
    return jax.shard_map(
        functools.partial(local, n_gx // NZ, NZ, ny),
        mesh=mesh,
        in_specs=(
            P("gx", "gy", None, None),
            P("gx", "gy", None, None),
            P("gx", "gy", None, None),
            P("gx", "gy", None, None),
            P("gx", "gy", None, None),
            P("gx", "gy", None),
        ),
        out_specs=P("gx", "gy", None, None),
        check_vma=False,
    )
```

```python
import functools

import jax
import jax.numpy as jnp
from jax import lax
from jax.experimental import pallas as pl
from jax.experimental.pallas import tpu as pltpu
from jax.sharding import PartitionSpec as P

NZ = 16
MESH = pl.DeviceIdType.MESH
F32 = jnp.float32
BF16 = jnp.bfloat16
HI = lax.Precision.HIGHEST


def mm(a, b):
    return jnp.dot(a, b, precision=HI, preferred_element_type=F32)


def mm_tn(a, b):
    return lax.dot_general(
        a, b, (((0,), (0,)), ((), ())), precision=HI, preferred_element_type=F32
    )


def iota(shape, dim):
    return lax.broadcasted_iota(jnp.int32, shape, dim)


def split3(v):
    hi = v.astype(BF16)
    rest = v - hi.astype(F32)
    mid = rest.astype(BF16)
    return hi, mid, (rest - mid.astype(F32)).astype(BF16)


def fill_lanes(big):
    spot = iota(big.shape, 0) - 128 == iota(big.shape, 1) // 128
    big[...] = jnp.where(spot, 1.0, 0.0).astype(BF16)


def eliminate(a_ref, g_ref, big, pad):
    sub = iota((8, 128), 0)

    def row(v, s):
        return jnp.broadcast_to(v[s : s + 1, :], (8, 128))

    pad[...] = jnp.zeros(pad.shape, F32)

    def step(i, carry):
        at = pl.multiple_of(i * 16, 16)
        here = pl.ds(at, 16)
        ra = a_ref[here, :]
        rg = g_ref[here, :]
        pick = big[pl.ds(pl.multiple_of(128 - at, 16), 128), :]
        spread = jnp.dot(
            jnp.concatenate(split3(ra), axis=0), pick, preferred_element_type=F32
        )
        spread = spread[0:16] + spread[16:32] + spread[32:48]
        lanes = [
            [spread[8 * h : 8 * h + 8, 128 * j : 128 * j + 128] for h in range(2)]
            for j in range(16)
        ]
        sides = [[ra[0:8], ra[8:16]], [rg[0:8], rg[8:16]]]
        scale = [jnp.ones((8, 128), F32)] * 2
        for k in range(16):
            h, s = divmod(k, 8)
            inv = 1.0 / row(lanes[k][h], s)
            factor = [lanes[k][0] * inv, lanes[k][1] * inv]
            factor[h] = jnp.where(sub == s, 0.0, factor[h])
            scale[h] = jnp.where(sub == s, inv, scale[h])
            for col in lanes[k + 1 :] + sides:
                pivot_row = row(col[h], s)
                for q in range(2):
                    col[q] = col[q] - factor[q] * pivot_row
        pa = jnp.concatenate([sides[0][0] * scale[0], sides[0][1] * scale[1]], axis=0)
        pg = jnp.concatenate([sides[1][0] * scale[0], sides[1][1] * scale[1]], axis=0)
        pad[here, 0:128] = pa
        pad[here, 128:256] = pg
        change = mm(a_ref[...], pad[...])
        a_ref[...] = a_ref[...] - change[:, 0:128]
        g_ref[...] = g_ref[...] - change[:, 128:256]
        a_ref[here, :] = pa
        g_ref[here, :] = pg
        pad[here, :] = jnp.zeros((16, 256), F32)
        return carry

    lax.fori_loop(0, 8, step, 0)


def kernel(
    nx, nz, ny,
    loads_hbm, schur_hbm, linv_hbm, basis_hbm, cinv_hbm, map_hbm,
    out_ref,
    loads_ref, schur_ref, linv_ref, basis_ref, cinv_ref, map_ref, insem,
    mp, sp, lf, xr, basis8, c8, cs, c2, cinb, zg, ps, pr, wcs, ims, imgs,
    res, sch, loc, dirs, upd,
    gsrc, gparts, gmine, gline, gtotal, gresult,
    ga, gb, gc, gd, ge, cval, big, pad,
    xsend, xrecv, psend, precv,
):
    ni, cols = loads_ref.shape
    face = ni // 4
    n_plane = nx * ny
    gx = lax.axis_index("gx")
    gy = lax.axis_index("gy")
    x = gx // nz
    z = lax.rem(gx, nz)
    me = x * ny + gy
    n_gx = nx * nz
    nyc = ny // 2

    def plane_id(q):
        return ((q // ny) * nz + z, lax.rem(q, ny))

    def line_id(k):
        return (x * nz + k, gy)

    exists = [gx > 0, gx < n_gx - 1, gy > 0, gy < ny - 1]
    nbr = [(gx - 1, gy), (gx + 1, gy), (gx, gy - 1), (gx, gy + 1)]
    w = [jnp.where(e, 0.5, 1.0).astype(F32) for e in exists]

    arrivals = [
        pltpu.make_async_copy(source, target, insem.at[i])
        for i, (source, target) in enumerate((
            (loads_hbm, loads_ref), (cinv_hbm, cinv_ref), (basis_hbm, basis_ref),
            (map_hbm, map_ref), (linv_hbm, linv_ref), (schur_hbm, schur_ref),
        ))
    ]
    for copy in arrivals:
        copy.start()

    barrier = pltpu.get_barrier_semaphore()

    def greet_line(o, carry):
        k = lax.rem(z + o, nz)
        pl.semaphore_signal(barrier, inc=1, device_id=line_id(k), device_id_type=MESH)
        return carry

    def greet_plane(o, carry):
        q = lax.rem(me + o, n_plane)
        pl.semaphore_signal(barrier, inc=1, device_id=plane_id(q), device_id_type=MESH)
        return carry

    lax.fori_loop(1, nz, greet_line, 0)
    lax.fori_loop(1, n_plane, greet_plane, 0)
    for f in range(2):
        @pl.when(exists[f])
        def _():
            pl.semaphore_signal(barrier, inc=1, device_id=nbr[f], device_id_type=MESH)

    fill_lanes(big)
    for copy in arrivals[:4]:
        copy.wait()
    lf[...] = loads_ref[...].astype(F32)
    for f in range(4):
        @pl.when(jnp.logical_not(exists[f]))
        def _():
            for ph in range(4):
                xr[ph, f] = jnp.zeros((face, cols), F32)
    basis8[...] = jnp.zeros(basis8.shape, F32)
    basis8[0:4, :] = basis_ref[...]
    c8[...] = jnp.zeros(c8.shape, F32)
    c8[0:4, :] = cinv_ref[...]
    if nz < 16:
        zg[...] = jnp.zeros(zg.shape, F32)

    width = nz * ny * 4
    slab = jnp.concatenate([c8[:, i * width : (i + 1) * width] for i in range(nx)], axis=0)
    parts = jnp.concatenate(split3(slab), axis=0)
    src = iota((width, 128), 0)
    dst = iota((width, 128), 1)
    src_z, src_y, src_b = src // (ny * 4), lax.rem(src // 4, ny), lax.rem(src, 4)
    want = jnp.where(src_z * 8 + src_b == dst, src_y, -1)
    for q in range(ny):
        pick = jnp.where(want == q, 1.0, 0.0).astype(BF16)
        moved = jnp.dot(parts, pick, preferred_element_type=F32)
        h = 8 * nx
        moved = moved[0:h] + moved[h : 2 * h] + moved[2 * h : 3 * h]
        for i in range(nx):
            cs[i * ny + q] = moved[8 * i : 8 * i + 8]

    onehot = jnp.where(iota((ni, ni), 0) == map_ref[...], 1.0, 0.0).astype(BF16)

    def permuted(matrix):
        right = lax.dot_general(
            matrix, onehot, (((1,), (1,)), ((), ())), preferred_element_type=F32
        ).astype(BF16)
        return jnp.dot(onehot, right, preferred_element_type=F32).astype(BF16)

    arrivals[4].wait()
    mp[...] = permuted(linv_ref[...])
    arrivals[5].wait()
    sp[...] = permuted(schur_ref[...])

    greeted = (nz - 1) + (n_plane - 1) + exists[0].astype(jnp.int32) + exists[1].astype(jnp.int32)
    pl.semaphore_wait(barrier, greeted)

    def face_copy(ph, f, source):
        return pltpu.make_async_remote_copy(
            src_ref=source.at[pl.ds(f * face, face)],
            dst_ref=xr.at[ph, f ^ 1],
            send_sem=xsend.at[ph, f],
            recv_sem=xrecv.at[ph, f ^ 1],
            device_id=nbr[f],
            device_id_type=MESH,
        )

    def face_arrival(ph, f, source):
        return pltpu.make_async_remote_copy(
            src_ref=source.at[pl.ds(f * face, face)],
            dst_ref=xr.at[ph, f],
            send_sem=xsend.at[ph, f],
            recv_sem=xrecv.at[ph, f],
            device_id=nbr[f],
            device_id_type=MESH,
        )

    def faces_start(ph, source):
        for f in range(4):
            @pl.when(exists[f])
            def _():
                face_copy(ph, f, source).start()

    def faces_wait(ph, source):
        for f in range(4):
            @pl.when(exists[f])
            def _():
                face_arrival(ph, f, source).wait_recv()

    def faces_sent(ph, source):
        for f in range(4):
            @pl.when(exists[f])
            def _():
                face_copy(ph, f, source).wait_send()

    def rows(f):
        return slice(f * face, (f + 1) * face)

    def wrap(v, n):
        return lax.rem(v, n)

    core = lax.rem(gy, 2)
    chip_y = gy // 2
    ys = [wrap(chip_y + o, nyc) for o in range(nyc)]
    far_y = [nyc // 2] + [o for o in range(nyc) if o not in (0, nyc // 2)] + [0]
    far_y = far_y if nyc > 1 else [0]

    def over_plane(send):
        def one(k, carry):
            xo = wrap(x + 1 + k, nx)
            for o in far_y:
                for d in (1, 0):
                    send(xo, ys[o], wrap(core + d, 2))
            return carry

        lax.fori_loop(0, nx - 1, one, 0)
        for o in far_y:
            for d in (1, 0):
                if o or d:
                    send(x, ys[o], wrap(core + d, 2))

    def over_chips(send):
        def one(k, carry):
            xo = wrap(x + 1 + k, nx)
            for o in far_y:
                send(xo, ys[o])
            return carry

        lax.fori_loop(0, nx - 1, one, 0)
        for o in far_y:
            if o:
                send(x, ys[o])

    def over_line(send):
        send(wrap(z + nz // 2, nz))

        def one(k, carry):
            d = nz // 2 - 1 - k
            send(wrap(z + d, nz))
            send(wrap(z + nz - d, nz))
            return carry

        lax.fori_loop(0, nz // 2 - 1, one, 0)

    def push(t, source, target, device):
        pltpu.make_async_remote_copy(
            src_ref=source, dst_ref=target,
            send_sem=psend.at[t], recv_sem=precv.at[t],
            device_id=device, device_id_type=MESH,
        ).start()

    def scatter_plane(t, source, target):
        target[me] = source[me]

        def send(xo, yo, co):
            q = xo * ny + yo * 2 + co
            push(t, source.at[q], target.at[me], (xo * nz + z, yo * 2 + co))

        over_plane(send)

    def spread_line(t, source, target):
        target[z] = source[...]
        over_line(lambda k: push(t, source, target.at[z], (x * nz + k, gy)))

    def arrived(t, target, n):
        part = target.at[pl.ds(0, n)]
        pltpu.make_async_copy(part, part, precv.at[t]).wait()

    def sent(t, target, n):
        part = target.at[pl.ds(0, n)]
        pltpu.make_async_copy(part, part, psend.at[t]).wait()

    n_tiles = n_plane // 2
    my_tile = x * nyc + chip_y

    class Sum:
        def __init__(self, r, parity):
            self.t = 5 + 3 * r
            self.parity = parity
            self.src, self.parts = gsrc.at[r], gparts.at[r]
            self.mine, self.line_parts = gmine.at[r], gline.at[r]
            self.total, self.result = gtotal.at[r], gresult.at[r]
            self.owner = core == parity

        def scatter(self, matrix):
            self.src[...] = matrix.reshape(n_tiles, 128 // n_tiles, 128)

            @pl.when(self.owner)
            def _():
                self.parts[me] = self.src[my_tile]

            def send(xo, yo):
                push(
                    self.t, self.src.at[xo * nyc + yo], self.parts.at[me],
                    (xo * nz + z, yo * 2 + self.parity),
                )

            over_chips(send)

            @pl.when(jnp.logical_not(self.owner))
            def _():
                send(x, chip_y)

        def line(self):
            @pl.when(self.owner)
            def _():
                arrived(self.t, self.parts, n_plane - 1)
                self.mine[...] = sum_rows(self.parts)
                spread_line(self.t + 1, self.mine, self.line_parts)

        def spread(self):
            @pl.when(self.owner)
            def _():
                arrived(self.t + 1, self.line_parts, nz - 1)
                self.total[...] = sum_rows(self.line_parts)
                self.result[my_tile] = self.total[...]
                over_plane(
                    lambda xo, yo, co: push(
                        self.t + 2, self.total, self.result.at[my_tile],
                        (xo * nz + z, yo * 2 + co),
                    )
                )

        def finish(self):
            @pl.when(self.owner)
            def _():
                if n_tiles > 1:
                    arrived(self.t + 2, self.result, n_tiles - 1)

            @pl.when(jnp.logical_not(self.owner))
            def _():
                arrived(self.t + 2, self.result, n_tiles)

            return self.result[...].reshape(128, 128)

        def drain(self):
            @pl.when(self.owner)
            def _():
                sent(self.t, self.parts, n_tiles - 1)
                sent(self.t + 1, self.line_parts, nz - 1)
                sent(self.t + 2, self.parts, n_plane - 1)

            @pl.when(jnp.logical_not(self.owner))
            def _():
                sent(self.t, self.parts, n_tiles)

    def sum_rows(ref):
        return jnp.sum(ref[...], axis=0)

    def coarse_send(it):
        cinb[it] = mm(basis8[...], sch[...])
        spread_line(1 + 2 * it, cinb.at[it], zg.at[it])

    def coarse_turn(it):
        arrived(1 + 2 * it, zg.at[it], nz - 1)
        gathered = zg[it].reshape(zg.shape[1] * 8, cols)
        partial = mm(c2[...].reshape(n_plane * 8, 128), gathered)
        ps[it] = partial.reshape(n_plane, 8, cols)
        scatter_plane(2 + 2 * it, ps.at[it], pr.at[it])

    def coarse_values(it):
        arrived(2 + 2 * it, pr.at[it], n_plane - 1)
        return sum_rows(pr.at[it])

    def correct(it, values):
        loc[...] = loc[...] + mm_tn(basis8[...], values)
        for f in range(4):
            wcs[it, rows(f), :] = w[f] * loc[rows(f), :]
        faces_start(1 + 2 * it, wcs.at[it])

    def symmetric(v):
        return 0.5 * (v + v.T)

    first_gram, first_curv = Sum(0, 0), Sum(1, 1)
    next_gram, cross_gram, own_curv = Sum(2, 0), Sum(3, 1), Sum(4, 0)

    faces_start(0, lf)
    faces_wait(0, lf)
    for f in range(4):
        res[rows(f), :] = lf[rows(f), :] + xr[0, f]
        sch[rows(f), :] = w[f] * res[rows(f), :]
    coarse_send(0)
    scatter_plane(0, cs, c2)
    loc[...] = jnp.dot(mp[...], sch[...].astype(BF16), preferred_element_type=F32)
    arrived(0, c2, n_plane - 1)
    coarse_turn(0)
    values0 = coarse_values(0)
    correct(0, values0)
    cval[...] = values0
    first_gram.scatter(mm_tn(sch[...], loc[...]))
    faces_wait(1, wcs.at[0])
    for f in range(4):
        dirs[rows(f), :] = wcs[0, rows(f), :] + xr[1, f]
    ims[...] = jnp.dot(sp[...], dirs[...].astype(BF16), preferred_element_type=F32)
    first_curv.scatter(mm_tn(dirs[...], ims[...]))
    faces_start(2, ims)

    first_gram.line()
    first_curv.line()
    faces_wait(2, ims)
    for f in range(4):
        imgs[rows(f), :] = ims[rows(f), :] + xr[2, f]
        sch[rows(f), :] = w[f] * imgs[rows(f), :]
    coarse_send(1)
    first_gram.spread()
    first_curv.spread()
    coarse_turn(1)
    gram0 = first_gram.finish()
    gb[...] = gram0
    ge[...] = symmetric(gram0)
    gc[...] = jnp.where(iota((128, 128), 0) == iota((128, 128), 1), 1.0, 0.0).astype(F32)
    half_curv = symmetric(first_curv.finish())
    gd[...] = half_curv
    ga[...] = half_curv
    eliminate(ga, gb, big, pad)
    image_values = coarse_values(1)
    alpha = gb[...]

    res[...] = res[...] - mm(imgs[...], alpha)
    for f in range(4):
        sch[rows(f), :] = w[f] * res[rows(f), :]
    loc[...] = jnp.dot(mp[...], sch[...].astype(BF16), preferred_element_type=F32)
    correct(1, cval[...] - mm(image_values, alpha))
    next_gram.scatter(mm_tn(sch[...], loc[...]))
    cross_gram.scatter(mm_tn(wcs[1], imgs[...]))
    faces_wait(3, wcs.at[1])
    for f in range(4):
        upd[rows(f), :] = wcs[1, rows(f), :] + xr[3, f]
    loc[...] = jnp.dot(sp[...], upd[...].astype(BF16), preferred_element_type=F32)
    own_curv.scatter(mm_tn(upd[...], loc[...]))
    next_gram.line()
    cross_gram.line()
    own_curv.line()
    eliminate(ge, gc, big, pad)
    next_gram.spread()
    cross_gram.spread()
    own_curv.spread()

    gram1 = next_gram.finish()
    ratio = mm(gc[...], gram1)
    known = mm_tn(ratio, mm(gd[...], ratio))
    step1 = gb[...]
    gb[...] = gram1
    side = mm(cross_gram.finish(), ratio)
    ga[...] = symmetric(own_curv.finish() + side + side.T + known)
    eliminate(ga, gb, big, pad)
    step2 = gb[...]
    step1 = step1 + mm(ratio, step2)
    out_ref[...] = mm(dirs[...], step1) + mm(upd[...], step2)

    for ph, source in enumerate((lf, wcs.at[0], ims, wcs.at[1])):
        faces_sent(ph, source)
    for it in range(2):
        sent(1 + 2 * it, zg.at[it], nz - 1)
        sent(2 + 2 * it, pr.at[it], n_plane - 1)
    sent(0, c2, n_plane - 1)
    for item in (first_gram, first_curv, next_gram, cross_gram, own_curv):
        item.drain()


def local(nx, nz, ny, loads, schur, local_inverse, coarse_basis, coarse_inverse, face_map):
    ni, cols = loads.shape[2:]
    n_plane = nx * ny
    vm = lambda *shape: pltpu.VMEM(shape, F32)
    face = ni // 4
    n_tiles = n_plane // 2
    tile = 128 // n_tiles
    zslots = max(nz, 16)
    scratch = [
        pltpu.VMEM((ni, cols), BF16), pltpu.VMEM((ni, ni), BF16), pltpu.VMEM((ni, ni), BF16),
        vm(4, ni), vm(4, coarse_inverse.shape[3]), pltpu.VMEM((1, ni), jnp.int32),
        pltpu.SemaphoreType.DMA((6,)),
        pltpu.VMEM((ni, ni), BF16), pltpu.VMEM((ni, ni), BF16),
        vm(ni, cols), vm(4, 4, face, cols),
        vm(8, ni), vm(8, coarse_inverse.shape[3]),
        vm(n_plane, 8, 128), vm(n_plane, 8, 128),
        vm(2, 8, cols), vm(2, zslots, 8, cols),
        vm(2, n_plane, 8, cols), vm(2, n_plane, 8, cols),
        vm(2, ni, cols), vm(ni, cols), vm(ni, cols),
        vm(ni, cols), vm(ni, cols), vm(ni, cols), vm(ni, cols), vm(ni, cols),
    ]
    scratch += [
        vm(5, n_tiles, tile, cols), vm(5, n_plane, tile, cols), vm(5, tile, cols),
        vm(5, nz, tile, cols), vm(5, tile, cols), vm(5, n_tiles, tile, cols),
    ]
    scratch += [vm(128, 128)] * 5 + [vm(8, cols), pltpu.VMEM((256, 2048), BF16), vm(128, 256)]
    scratch += [
        pltpu.SemaphoreType.DMA((4, 4)), pltpu.SemaphoreType.DMA((4, 4)),
        pltpu.SemaphoreType.DMA((20,)), pltpu.SemaphoreType.DMA((20,)),
    ]
    vmem = pl.BlockSpec(memory_space=pltpu.VMEM)
    out = pl.pallas_call(
        functools.partial(kernel, nx, nz, ny),
        out_shape=jax.ShapeDtypeStruct((ni, cols), F32),
        in_specs=[pl.BlockSpec(memory_space=pltpu.HBM)] * 6,
        out_specs=vmem,
        scratch_shapes=scratch,
        compiler_params=pltpu.CompilerParams(
            collective_id=0, has_side_effects=True, vmem_limit_bytes=67_000_000
        ),
        name="bddc",
    )(
        loads[0, 0], schur[0, 0], local_inverse[0, 0], coarse_basis[0, 0],
        coarse_inverse[0, 0], face_map[0],
    )
    return out[None, None]


def solution(mesh):
    n_gx, ny = mesh.shape["gx"], mesh.shape["gy"]
    return jax.shard_map(
        functools.partial(local, n_gx // NZ, NZ, ny),
        mesh=mesh,
        in_specs=(
            P("gx", "gy", None, None),
            P("gx", "gy", None, None),
            P("gx", "gy", None, None),
            P("gx", "gy", None, None),
            P("gx", "gy", None, None),
            P("gx", "gy", None),
        ),
        out_specs=P("gx", "gy", None, None),
        check_vma=False,
    )
```

```python
import functools

import jax
import jax.numpy as jnp
from jax import lax
from jax.experimental import pallas as pl
from jax.experimental.pallas import tpu as pltpu
from jax.sharding import PartitionSpec as P

NZ = 16
MESH = pl.DeviceIdType.MESH
F32 = jnp.float32
BF16 = jnp.bfloat16
HI = lax.Precision.HIGHEST


def mm(a, b):
    return jnp.dot(a, b, precision=HI, preferred_element_type=F32)


def mm_tn(a, b):
    return lax.dot_general(
        a, b, (((0,), (0,)), ((), ())), precision=HI, preferred_element_type=F32
    )


def iota(shape, dim):
    return lax.broadcasted_iota(jnp.int32, shape, dim)


def split3(v):
    hi = v.astype(BF16)
    rest = v - hi.astype(F32)
    mid = rest.astype(BF16)
    return hi, mid, (rest - mid.astype(F32)).astype(BF16)


def fill_lanes(big):
    spot = iota(big.shape, 0) - 128 == iota(big.shape, 1) // 128
    big[...] = jnp.where(spot, 1.0, 0.0).astype(BF16)


def eliminate(a_ref, g_ref, big, pad):
    sub = iota((8, 128), 0)

    def row(v, s):
        return jnp.broadcast_to(v[s : s + 1, :], (8, 128))

    pad[...] = jnp.zeros(pad.shape, F32)

    def step(i, carry):
        at = pl.multiple_of(i * 16, 16)
        here = pl.ds(at, 16)
        ra = a_ref[here, :]
        rg = g_ref[here, :]
        pick = big[pl.ds(pl.multiple_of(128 - at, 16), 128), :]
        spread = jnp.dot(
            jnp.concatenate(split3(ra), axis=0), pick, preferred_element_type=F32
        )
        spread = spread[0:16] + spread[16:32] + spread[32:48]
        lanes = [
            [spread[8 * h : 8 * h + 8, 128 * j : 128 * j + 128] for h in range(2)]
            for j in range(16)
        ]
        sides = [[ra[0:8], ra[8:16]], [rg[0:8], rg[8:16]]]
        scale = [jnp.ones((8, 128), F32)] * 2
        for k in range(16):
            h, s = divmod(k, 8)
            inv = 1.0 / row(lanes[k][h], s)
            factor = [lanes[k][0] * inv, lanes[k][1] * inv]
            factor[h] = jnp.where(sub == s, 0.0, factor[h])
            scale[h] = jnp.where(sub == s, inv, scale[h])
            for col in lanes[k + 1 :] + sides:
                pivot_row = row(col[h], s)
                for q in range(2):
                    col[q] = col[q] - factor[q] * pivot_row
        pa = jnp.concatenate([sides[0][0] * scale[0], sides[0][1] * scale[1]], axis=0)
        pg = jnp.concatenate([sides[1][0] * scale[0], sides[1][1] * scale[1]], axis=0)
        pad[here, 0:128] = pa
        pad[here, 128:256] = pg
        change = mm(a_ref[...], pad[...])
        a_ref[...] = a_ref[...] - change[:, 0:128]
        g_ref[...] = g_ref[...] - change[:, 128:256]
        a_ref[here, :] = pa
        g_ref[here, :] = pg
        pad[here, :] = jnp.zeros((16, 256), F32)
        return carry

    lax.fori_loop(0, 8, step, 0)


def kernel(
    nx, nz, ny,
    loads_hbm, schur_hbm, linv_hbm, basis_hbm, cinv_hbm, map_hbm,
    out_ref,
    loads_ref, schur_ref, linv_ref, basis_ref, cinv_ref, map_ref, insem,
    mp, sp, lf, xr, basis8, c8, cs, c2, cinb, zg, ps, pr, wcs, ims, imgs,
    res, sch, loc, dirs, upd,
    gsrc, gparts, gmine, gline, gtotal, gresult,
    ga, gb, gc, gd, ge, cval, big, pad,
    xsend, xrecv, psend, precv,
):
    ni, cols = loads_ref.shape
    face = ni // 4
    n_plane = nx * ny
    gx = lax.axis_index("gx")
    gy = lax.axis_index("gy")
    x = gx // nz
    z = lax.rem(gx, nz)
    me = x * ny + gy
    n_gx = nx * nz
    nyc = ny // 2

    def plane_id(q):
        return ((q // ny) * nz + z, lax.rem(q, ny))

    def line_id(k):
        return (x * nz + k, gy)

    exists = [gx > 0, gx < n_gx - 1, gy > 0, gy < ny - 1]
    nbr = [(gx - 1, gy), (gx + 1, gy), (gx, gy - 1), (gx, gy + 1)]
    w = [jnp.where(e, 0.5, 1.0).astype(F32) for e in exists]

    arrivals = [
        pltpu.make_async_copy(source, target, insem.at[i])
        for i, (source, target) in enumerate((
            (loads_hbm, loads_ref), (cinv_hbm, cinv_ref), (basis_hbm, basis_ref),
            (map_hbm, map_ref), (linv_hbm, linv_ref), (schur_hbm, schur_ref),
        ))
    ]
    for copy in arrivals:
        copy.start()

    for target in (zg, pr, c2):
        target[...] = jnp.zeros(target.shape, F32)

    barrier = pltpu.get_barrier_semaphore()

    def greet_line(o, carry):
        k = lax.rem(z + o, nz)
        pl.semaphore_signal(barrier, inc=1, device_id=line_id(k), device_id_type=MESH)
        return carry

    def greet_plane(o, carry):
        q = lax.rem(me + o, n_plane)
        pl.semaphore_signal(barrier, inc=1, device_id=plane_id(q), device_id_type=MESH)
        return carry

    lax.fori_loop(1, nz, greet_line, 0)
    lax.fori_loop(1, n_plane, greet_plane, 0)
    for f in range(2):
        @pl.when(exists[f])
        def _():
            pl.semaphore_signal(barrier, inc=1, device_id=nbr[f], device_id_type=MESH)

    fill_lanes(big)
    for copy in arrivals[:4]:
        copy.wait()
    lf[...] = loads_ref[...].astype(F32)
    for f in range(4):
        @pl.when(jnp.logical_not(exists[f]))
        def _():
            for ph in range(4):
                xr[ph, f] = jnp.zeros((face, cols), F32)
    basis8[...] = jnp.zeros(basis8.shape, F32)
    basis8[0:4, :] = basis_ref[...]
    c8[...] = jnp.zeros(c8.shape, F32)
    c8[0:4, :] = cinv_ref[...]

    width = nz * ny * 4
    slab = jnp.concatenate([c8[:, i * width : (i + 1) * width] for i in range(nx)], axis=0)
    parts = jnp.concatenate(split3(slab), axis=0)
    src = iota((width, 128), 0)
    dst = iota((width, 128), 1)
    src_z, src_y, src_b = src // (ny * 4), lax.rem(src // 4, ny), lax.rem(src, 4)
    want = jnp.where(src_z * 8 + src_b == dst, src_y, -1)
    for q in range(ny):
        pick = jnp.where(want == q, 1.0, 0.0).astype(BF16)
        moved = jnp.dot(parts, pick, preferred_element_type=F32)
        h = 8 * nx
        moved = moved[0:h] + moved[h : 2 * h] + moved[2 * h : 3 * h]
        for i in range(nx):
            cs[i * ny + q] = moved[8 * i : 8 * i + 8]

    onehot = jnp.where(iota((ni, ni), 0) == map_ref[...], 1.0, 0.0).astype(BF16)

    def permuted(matrix):
        right = lax.dot_general(
            matrix, onehot, (((1,), (1,)), ((), ())), preferred_element_type=F32
        ).astype(BF16)
        return jnp.dot(onehot, right, preferred_element_type=F32).astype(BF16)

    arrivals[4].wait()
    mp[...] = permuted(linv_ref[...])
    arrivals[5].wait()
    sp[...] = permuted(schur_ref[...])

    greeted = (nz - 1) + (n_plane - 1) + exists[0].astype(jnp.int32) + exists[1].astype(jnp.int32)
    pl.semaphore_wait(barrier, greeted)

    def face_copy(ph, f, source):
        return pltpu.make_async_remote_copy(
            src_ref=source.at[pl.ds(f * face, face)],
            dst_ref=xr.at[ph, f ^ 1],
            send_sem=xsend.at[ph, f],
            recv_sem=xrecv.at[ph, f ^ 1],
            device_id=nbr[f],
            device_id_type=MESH,
        )

    def face_arrival(ph, f, source):
        return pltpu.make_async_remote_copy(
            src_ref=source.at[pl.ds(f * face, face)],
            dst_ref=xr.at[ph, f],
            send_sem=xsend.at[ph, f],
            recv_sem=xrecv.at[ph, f],
            device_id=nbr[f],
            device_id_type=MESH,
        )

    def faces_start(ph, source):
        for f in range(4):
            @pl.when(exists[f])
            def _():
                face_copy(ph, f, source).start()

    def faces_wait(ph, source):
        for f in range(4):
            @pl.when(exists[f])
            def _():
                face_arrival(ph, f, source).wait_recv()

    def faces_sent(ph, source):
        for f in range(4):
            @pl.when(exists[f])
            def _():
                face_copy(ph, f, source).wait_send()

    def rows(f):
        return slice(f * face, (f + 1) * face)

    def wrap(v, n):
        return lax.rem(v, n)

    core = lax.rem(gy, 2)
    chip_y = gy // 2
    ys = [wrap(chip_y + o, nyc) for o in range(nyc)]
    far_y = [nyc // 2] + [o for o in range(nyc) if o not in (0, nyc // 2)] + [0]
    far_y = far_y if nyc > 1 else [0]

    def over_plane(send):
        def one(k, carry):
            xo = wrap(x + 1 + k, nx)
            for o in far_y:
                for d in (1, 0):
                    send(xo, ys[o], wrap(core + d, 2))
            return carry

        lax.fori_loop(0, nx - 1, one, 0)
        for o in far_y:
            for d in (1, 0):
                if o or d:
                    send(x, ys[o], wrap(core + d, 2))

    def over_chips(send):
        def one(k, carry):
            xo = wrap(x + 1 + k, nx)
            for o in far_y:
                send(xo, ys[o])
            return carry

        lax.fori_loop(0, nx - 1, one, 0)
        for o in far_y:
            if o:
                send(x, ys[o])

    def over_line(send):
        send(wrap(z + nz // 2, nz))

        def one(k, carry):
            d = nz // 2 - 1 - k
            send(wrap(z + d, nz))
            send(wrap(z + nz - d, nz))
            return carry

        lax.fori_loop(0, nz // 2 - 1, one, 0)

    def push(t, source, target, device):
        pltpu.make_async_remote_copy(
            src_ref=source, dst_ref=target,
            send_sem=psend.at[t], recv_sem=precv.at[t],
            device_id=device, device_id_type=MESH,
        ).start()

    def scatter_plane(t, source, target):
        target[me] = source[me]
        some = pl.ds(0, 4)

        def send(xo, yo, co):
            q = xo * ny + yo * 2 + co
            push(t, source.at[q, some], target.at[me, some], (xo * nz + z, yo * 2 + co))

        over_plane(send)

    def spread_line(t, source, target, n_rows):
        target[z] = source[...]
        some = pl.ds(0, n_rows)
        over_line(
            lambda k: push(t, source.at[some], target.at[z, some], (x * nz + k, gy))
        )

    def arrived(t, target, n, n_rows):
        part = target.at[pl.ds(0, n), pl.ds(0, n_rows)]
        pltpu.make_async_copy(part, part, precv.at[t]).wait()

    def sent(t, target, n, n_rows):
        part = target.at[pl.ds(0, n), pl.ds(0, n_rows)]
        pltpu.make_async_copy(part, part, psend.at[t]).wait()

    n_tiles = n_plane // 2
    tile = 128 // n_tiles
    my_tile = x * nyc + chip_y

    class Sum:
        def __init__(self, r, parity):
            self.t = 5 + 3 * r
            self.parity = parity
            self.src, self.parts = gsrc.at[r], gparts.at[r]
            self.mine, self.line_parts = gmine.at[r], gline.at[r]
            self.total, self.result = gtotal.at[r], gresult.at[r]
            self.owner = core == parity

        def scatter(self, matrix):
            self.src[...] = matrix.reshape(n_tiles, 128 // n_tiles, 128)

            @pl.when(self.owner)
            def _():
                self.parts[me] = self.src[my_tile]

            def send(xo, yo):
                push(
                    self.t, self.src.at[xo * nyc + yo], self.parts.at[me],
                    (xo * nz + z, yo * 2 + self.parity),
                )

            over_chips(send)

            @pl.when(jnp.logical_not(self.owner))
            def _():
                send(x, chip_y)

        def line(self):
            @pl.when(self.owner)
            def _():
                arrived(self.t, self.parts, n_plane - 1, tile)
                self.mine[...] = sum_rows(self.parts)
                spread_line(self.t + 1, self.mine, self.line_parts, tile)

        def spread(self):
            @pl.when(self.owner)
            def _():
                arrived(self.t + 1, self.line_parts, nz - 1, tile)
                self.total[...] = sum_rows(self.line_parts)
                self.result[my_tile] = self.total[...]
                over_plane(
                    lambda xo, yo, co: push(
                        self.t + 2, self.total, self.result.at[my_tile],
                        (xo * nz + z, yo * 2 + co),
                    )
                )

        def finish(self):
            @pl.when(self.owner)
            def _():
                if n_tiles > 1:
                    arrived(self.t + 2, self.result, n_tiles - 1, tile)

            @pl.when(jnp.logical_not(self.owner))
            def _():
                arrived(self.t + 2, self.result, n_tiles, tile)

            return self.result[...].reshape(128, 128)

        def drain(self):
            @pl.when(self.owner)
            def _():
                sent(self.t, self.parts, n_tiles - 1, tile)
                sent(self.t + 1, self.line_parts, nz - 1, tile)
                sent(self.t + 2, self.parts, n_plane - 1, tile)

            @pl.when(jnp.logical_not(self.owner))
            def _():
                sent(self.t, self.parts, n_tiles, tile)

    def sum_rows(ref):
        return jnp.sum(ref[...], axis=0)

    def coarse_send(it):
        cinb[it] = mm(basis8[...], sch[...])
        spread_line(1 + 2 * it, cinb.at[it], zg.at[it], 4)

    def coarse_turn(it):
        arrived(1 + 2 * it, zg.at[it], nz - 1, 4)
        gathered = zg[it].reshape(zg.shape[1] * 8, cols)
        partial = mm(c2[...].reshape(n_plane * 8, 128), gathered)
        ps[it] = partial.reshape(n_plane, 8, cols)
        scatter_plane(2 + 2 * it, ps.at[it], pr.at[it])

    def coarse_values(it):
        arrived(2 + 2 * it, pr.at[it], n_plane - 1, 4)
        return sum_rows(pr.at[it])

    def correct(it, values):
        loc[...] = loc[...] + mm_tn(basis8[...], values)
        for f in range(4):
            wcs[it, rows(f), :] = w[f] * loc[rows(f), :]
        faces_start(1 + 2 * it, wcs.at[it])

    def symmetric(v):
        return 0.5 * (v + v.T)

    first_gram, first_curv = Sum(0, 0), Sum(1, 1)
    next_gram, cross_gram, own_curv = Sum(2, 0), Sum(3, 1), Sum(4, 0)

    faces_start(0, lf)
    faces_wait(0, lf)
    for f in range(4):
        res[rows(f), :] = lf[rows(f), :] + xr[0, f]
        sch[rows(f), :] = w[f] * res[rows(f), :]
    coarse_send(0)
    scatter_plane(0, cs, c2)
    loc[...] = jnp.dot(mp[...], sch[...].astype(BF16), preferred_element_type=F32)
    arrived(0, c2, n_plane - 1, 4)
    coarse_turn(0)
    values0 = coarse_values(0)
    correct(0, values0)
    cval[...] = values0
    first_gram.scatter(mm_tn(sch[...], loc[...]))
    faces_wait(1, wcs.at[0])
    for f in range(4):
        dirs[rows(f), :] = wcs[0, rows(f), :] + xr[1, f]
    ims[...] = jnp.dot(sp[...], dirs[...].astype(BF16), preferred_element_type=F32)
    first_curv.scatter(mm_tn(dirs[...], ims[...]))
    faces_start(2, ims)

    first_gram.line()
    first_curv.line()
    faces_wait(2, ims)
    for f in range(4):
        imgs[rows(f), :] = ims[rows(f), :] + xr[2, f]
        sch[rows(f), :] = w[f] * imgs[rows(f), :]
    coarse_send(1)
    first_gram.spread()
    first_curv.spread()
    coarse_turn(1)
    gram0 = first_gram.finish()
    gb[...] = gram0
    ge[...] = symmetric(gram0)
    gc[...] = jnp.where(iota((128, 128), 0) == iota((128, 128), 1), 1.0, 0.0).astype(F32)
    half_curv = symmetric(first_curv.finish())
    gd[...] = half_curv
    ga[...] = half_curv
    eliminate(ga, gb, big, pad)
    image_values = coarse_values(1)
    alpha = gb[...]

    res[...] = res[...] - mm(imgs[...], alpha)
    for f in range(4):
        sch[rows(f), :] = w[f] * res[rows(f), :]
    loc[...] = jnp.dot(mp[...], sch[...].astype(BF16), preferred_element_type=F32)
    correct(1, cval[...] - mm(image_values, alpha))
    next_gram.scatter(mm_tn(sch[...], loc[...]))
    cross_gram.scatter(mm_tn(wcs[1], imgs[...]))
    faces_wait(3, wcs.at[1])
    for f in range(4):
        upd[rows(f), :] = wcs[1, rows(f), :] + xr[3, f]
    loc[...] = jnp.dot(sp[...], upd[...].astype(BF16), preferred_element_type=F32)
    own_curv.scatter(mm_tn(upd[...], loc[...]))
    next_gram.line()
    cross_gram.line()
    own_curv.line()
    eliminate(ge, gc, big, pad)
    next_gram.spread()
    cross_gram.spread()
    own_curv.spread()

    gram1 = next_gram.finish()
    ratio = mm(gc[...], gram1)
    known = mm_tn(ratio, mm(gd[...], ratio))
    step1 = gb[...]
    gb[...] = gram1
    side = mm(cross_gram.finish(), ratio)
    ga[...] = symmetric(own_curv.finish() + side + side.T + known)
    eliminate(ga, gb, big, pad)
    step2 = gb[...]
    step1 = step1 + mm(ratio, step2)
    out_ref[...] = mm(dirs[...], step1) + mm(upd[...], step2)

    for ph, source in enumerate((lf, wcs.at[0], ims, wcs.at[1])):
        faces_sent(ph, source)
    for it in range(2):
        sent(1 + 2 * it, zg.at[it], nz - 1, 4)
        sent(2 + 2 * it, pr.at[it], n_plane - 1, 4)
    sent(0, c2, n_plane - 1, 4)
    for item in (first_gram, first_curv, next_gram, cross_gram, own_curv):
        item.drain()


def local(nx, nz, ny, loads, schur, local_inverse, coarse_basis, coarse_inverse, face_map):
    ni, cols = loads.shape[2:]
    n_plane = nx * ny
    vm = lambda *shape: pltpu.VMEM(shape, F32)
    face = ni // 4
    n_tiles = n_plane // 2
    tile = 128 // n_tiles
    zslots = max(nz, 16)
    scratch = [
        pltpu.VMEM((ni, cols), BF16), pltpu.VMEM((ni, ni), BF16), pltpu.VMEM((ni, ni), BF16),
        vm(4, ni), vm(4, coarse_inverse.shape[3]), pltpu.VMEM((1, ni), jnp.int32),
        pltpu.SemaphoreType.DMA((6,)),
        pltpu.VMEM((ni, ni), BF16), pltpu.VMEM((ni, ni), BF16),
        vm(ni, cols), vm(4, 4, face, cols),
        vm(8, ni), vm(8, coarse_inverse.shape[3]),
        vm(n_plane, 8, 128), vm(n_plane, 8, 128),
        vm(2, 8, cols), vm(2, zslots, 8, cols),
        vm(2, n_plane, 8, cols), vm(2, n_plane, 8, cols),
        vm(2, ni, cols), vm(ni, cols), vm(ni, cols),
        vm(ni, cols), vm(ni, cols), vm(ni, cols), vm(ni, cols), vm(ni, cols),
    ]
    scratch += [
        vm(5, n_tiles, tile, cols), vm(5, n_plane, tile, cols), vm(5, tile, cols),
        vm(5, nz, tile, cols), vm(5, tile, cols), vm(5, n_tiles, tile, cols),
    ]
    scratch += [vm(128, 128)] * 5 + [vm(8, cols), pltpu.VMEM((256, 2048), BF16), vm(128, 256)]
    scratch += [
        pltpu.SemaphoreType.DMA((4, 4)), pltpu.SemaphoreType.DMA((4, 4)),
        pltpu.SemaphoreType.DMA((20,)), pltpu.SemaphoreType.DMA((20,)),
    ]
    vmem = pl.BlockSpec(memory_space=pltpu.VMEM)
    out = pl.pallas_call(
        functools.partial(kernel, nx, nz, ny),
        out_shape=jax.ShapeDtypeStruct((ni, cols), F32),
        in_specs=[pl.BlockSpec(memory_space=pltpu.HBM)] * 6,
        out_specs=vmem,
        scratch_shapes=scratch,
        compiler_params=pltpu.CompilerParams(
            collective_id=0, has_side_effects=True, vmem_limit_bytes=67_000_000
        ),
        name="bddc",
    )(
        loads[0, 0], schur[0, 0], local_inverse[0, 0], coarse_basis[0, 0],
        coarse_inverse[0, 0], face_map[0],
    )
    return out[None, None]


def solution(mesh):
    n_gx, ny = mesh.shape["gx"], mesh.shape["gy"]
    return jax.shard_map(
        functools.partial(local, n_gx // NZ, NZ, ny),
        mesh=mesh,
        in_specs=(
            P("gx", "gy", None, None),
            P("gx", "gy", None, None),
            P("gx", "gy", None, None),
            P("gx", "gy", None, None),
            P("gx", "gy", None, None),
            P("gx", "gy", None),
        ),
        out_specs=P("gx", "gy", None, None),
        check_vma=False,
    )
```
